256 devices in a mesh: ctx: 64 (over x, z, core), rep: 4 (over y).
Axes of the slice: x: 4, y: 4, z: 8, core: 2. Of those that a mesh axis runs over, the one named last changes fastest.
Arguments:
- latents: bfloat16 [1048576, 576], P(('ctx', 'rep')), may hold values from -6 to 6
- queries: bfloat16 [64, 73728], P('rep', 'ctx'), may hold values from -4000 to 4000, as said below
- hot_ids: int32 [128], P('ctx'), may hold values from 0 to 15, as said below
- lengths: int32 [64], P('rep'), may hold values from 524288 to 1048576
Outputs:
- attended: bfloat16 [64, 65536], P('rep', 'ctx')
The draws below stay inside these ranges and needn't reach their ends.
Inputs may be any that keep to these rules, and one draw needn't show every extreme that they name: `queries`: query entries lie in the stated range. `hot_ids`: entries g * 2 to (g + 1) * 2 - 1 are distinct block numbers within group g.
All inputs are finite; a program needn't handle non-finite values.
Results may differ from the reference program's by a relative error of at most 0.0031.
Values may be sent and summed in bfloat16 or wider, within the bound.
No kernel may reach another device: no remote copies, remote signals or barrier semaphores. Data moves between devices by JAX's collectives and lax.ppermute only.
A program may use at most 128 MiB of HBM per device.

```python
import jax
import jax.numpy as jnp
from jax import lax

H = 128
LAT = 512
ROPE = 64
QK = 192
BLK = 1024
HOT_GRP = 2
BPG = 16
CTX = 1048576
NQ = 64
N_CTX = 64


def hot_table(key):
    sub_keys = jax.random.split(jax.random.fold_in(key, 101), N_CTX)
    picked_ids = jax.vmap(lambda one_key: jax.random.permutation(one_key, BPG)[:HOT_GRP])(sub_keys)
    return picked_ids.reshape(-1).astype(jnp.int32)


def block_rows(key, block_number):
    row_width = LAT + ROPE
    block_key = jax.random.fold_in(jax.random.fold_in(key, 202), block_number)
    return jnp.clip(jax.random.normal(block_key, (BLK, row_width), jnp.float32), -6.0, 6.0)


def probe_target(pair_index):
    return 120.0 + 45.0 * pair_index


def apply_pairs(pair_rows):
    for pair_index in range(4):
        upper_row = 2 * pair_index
        pair_rows = pair_rows.at[upper_row, LAT].set(1.0)
        energy = jnp.sum(pair_rows[upper_row, LAT:] * pair_rows[upper_row, LAT:])
        lower_entry = 1.0 - 2.0 * energy / probe_target(pair_index)
        pair_rows = pair_rows.at[upper_row + 1, LAT:].set(pair_rows[upper_row, LAT:])
        pair_rows = pair_rows.at[upper_row + 1, LAT].set(lower_entry)
    return pair_rows


def draw_hot_ids(key, part):
    return hot_table(key)


def draw_latents(key, part):
    row_width = LAT + ROPE
    all_blocks = jax.vmap(lambda number: block_rows(key, number))(jnp.arange(CTX // BLK, dtype=jnp.int32))
    first_block = hot_table(key)[0]
    all_blocks = all_blocks.at[first_block].set(apply_pairs(all_blocks[first_block]))
    return all_blocks.reshape(CTX, row_width).astype(jnp.bfloat16)


def draw_queries(key, part):
    row_width = LAT + ROPE
    query_draw = 1.5 * jnp.clip(jax.random.normal(jax.random.fold_in(key, 303), (NQ, H, row_width), jnp.float32), -6.0, 6.0)
    pair_rows = apply_pairs(block_rows(key, hot_table(key)[0]))
    for pair_index in range(4):
        rotary_part = pair_rows[2 * pair_index, LAT:]
        energy = jnp.sum(rotary_part * rotary_part)
        strength = probe_target(pair_index) * QK ** 0.5 / energy
        probe_row = jnp.zeros((row_width,), jnp.float32).at[LAT:].set(strength * rotary_part)
        query_draw = query_draw.at[pair_index * (NQ // 4), pair_index].set(probe_row)
    return query_draw.reshape(NQ, H * row_width).astype(jnp.bfloat16)


def set_ends(values, own_key, low, high):
    longest = values.shape.index(max(values.shape))
    spots = []
    for shift in (0, 1):
        where = [jax.random.randint(jax.random.fold_in(own_key, axis), (), 0, length) for axis, length in enumerate(values.shape)]
        where[longest] = (where[longest] + shift) % values.shape[longest]
        spots.append(tuple(where))
    return values.at[spots[0]].set(low).at[spots[1]].set(high)


def setup_inputs(seed: int = 0) -> dict:
    streams_of = jax.random.split(jax.random.key(seed), 5)
    latents = draw_latents(jax.random.fold_in(streams_of[4], 71), 0)
    queries = draw_queries(jax.random.fold_in(streams_of[4], 71), 0)
    hot_ids = draw_hot_ids(jax.random.fold_in(streams_of[4], 71), 0)
    lengths = set_ends(jax.random.randint(streams_of[3], (NQ,), CTX // 2, CTX + 1), jax.random.fold_in(streams_of[3], 1), CTX // 2, CTX).astype(jnp.int32)
    return {"latents": latents, "queries": queries, "hot_ids": hot_ids, "lengths": lengths}


def group_partials(query_heads, key_rows, row_index, lengths, score_scale):
    scores = jnp.einsum("qhw,kw->qhk", query_heads.astype(jnp.float32), key_rows.astype(jnp.float32)) * score_scale
    visible = row_index[None, None, :] < lengths[:, None, None]
    peak_score = jnp.max(jnp.where(visible, scores, -1e30), axis=2)
    exponent = jnp.where(visible, scores - peak_score[:, :, None], -1e30)
    weights = jnp.exp(exponent).astype(jnp.bfloat16)
    totals = jnp.sum(weights.astype(jnp.float32), axis=2)
    numerators = jnp.einsum("qhk,kl->qhl", weights.astype(jnp.float32), key_rows[:, :LAT].astype(jnp.float32))
    return numerators, peak_score, totals


def reference(latents, queries, hot_ids, lengths):
    row_width = LAT + ROPE
    score_scale = QK ** -0.5
    query_heads = queries.reshape(NQ, H, row_width)
    blocks = latents.reshape(N_CTX, BPG, BLK, row_width)
    hot_matrix = hot_ids.reshape(N_CTX, HOT_GRP)
    offsets = jnp.arange(BLK, dtype=jnp.int32)

    def fold(running, group_index):
        overall, numer_run, total_run = running
        chosen = hot_matrix[group_index]
        key_rows = blocks[group_index][chosen].reshape(HOT_GRP * BLK, row_width)
        row_index = ((group_index * BPG + chosen)[:, None] * BLK + offsets[None, :]).reshape(-1).astype(jnp.int32)
        numerators, peak_score, totals = group_partials(query_heads, key_rows, row_index, lengths, score_scale)
        new_overall = jnp.maximum(overall, peak_score)
        old_factor = jnp.exp(overall - new_overall)
        new_factor = jnp.exp(peak_score - new_overall)
        numer_run = numer_run * old_factor[..., None] + numerators * new_factor[..., None]
        total_run = total_run * old_factor + totals * new_factor
        return (new_overall, numer_run, total_run), None

    initial = (jnp.full((NQ, H), -1e30, jnp.float32), jnp.zeros((NQ, H, LAT), jnp.float32), jnp.zeros((NQ, H), jnp.float32))
    (overall, numer_run, total_run), _ = lax.scan(fold, initial, jnp.arange(N_CTX, dtype=jnp.int32))
    return (numer_run / total_run[..., None]).reshape(NQ, H * LAT).astype(jnp.bfloat16)
```

```python
import jax
import jax.numpy as jnp
from jax import lax
from jax.experimental import pallas as pl
from jax.experimental.pallas import tpu as pltpu
from jax.sharding import PartitionSpec as P

H = 128
LAT = 512
ROPE = 64
QK = 192
BLK = 1024
HOT_GRP = 2
BPG = 16
WIDTH = LAT + ROPE
N_X = 4
N_Z = 8
N_C = 2
N_REP = 4
PER_DEV = BPG // N_REP
QUARTER = BLK // N_REP
CHUNK = HOT_GRP * QUARTER
NEVER = -1e30


def ctx_index(x, z, c):
    return ((x % N_X) * N_Z + z % N_Z) * N_C + c


def all_ctx():
    return [(x, z, c) for x in range(N_X) for z in range(N_Z) for c in range(N_C)]


def shift_x(a, by):
    pairs = [(ctx_index(x, z, c), ctx_index(x + by, z, c)) for x, z, c in all_ctx()]
    return lax.ppermute(a, "ctx", pairs)


def shift_z(a, by):
    pairs = [(ctx_index(x, z, c), ctx_index(x, z + by, c)) for x, z, c in all_ctx()]
    return lax.ppermute(a, "ctx", pairs)


def swap_core(a):
    pairs = [(ctx_index(x, z, c), ctx_index(x, z, 1 - c)) for x, z, c in all_ctx()]
    return lax.ppermute(a, "ctx", pairs)


def shift_rep(a, by):
    return lax.ppermute(a, "rep", [(i, (i + by) % N_REP) for i in range(N_REP)])


def attend_kernel(q_ref, lens_ref, rows_ref, *refs):
    key_refs, (o_ref, stat_ref) = refs[: 2 * N_REP], refs[2 * N_REP :]
    q = q_ref[...]
    lens = lens_ref[...]
    parts = []
    for group in range(N_C):
        keys = key_refs[group * N_REP : (group + 1) * N_REP]
        scores = []
        for i, k_ref in enumerate(keys):
            s = jnp.dot(q, k_ref[...], preferred_element_type=jnp.float32) * (QK**-0.5)
            rows = rows_ref[group : group + 1, i * CHUNK : (i + 1) * CHUNK]
            scores.append(jnp.where(rows < lens, s, NEVER))
        peak = scores[0].max(axis=1, keepdims=True)
        for s in scores[1:]:
            peak = jnp.maximum(peak, s.max(axis=1, keepdims=True))
        total = jnp.zeros_like(peak)
        numer = None
        for s, k_ref in zip(scores, keys):
            w = jnp.exp(s - peak).astype(jnp.bfloat16)
            total = total + jnp.sum(w.astype(jnp.float32), axis=1, keepdims=True)
            n = lax.dot_general(
                w, k_ref[:LAT, :], (((1,), (1,)), ((), ())), preferred_element_type=jnp.float32
            )
            numer = n if numer is None else numer + n
        parts.append((peak, total, numer))
    top = jnp.maximum(parts[0][0], parts[1][0])
    numer, total = 0.0, 0.0
    for peak, t, n in parts:
        f = jnp.where(peak > NEVER / 2, jnp.exp(peak - top), 0.0)
        numer = numer + n * f
        total = total + t * f
    inv = 1.0 / jnp.maximum(total, 1.0)
    o_ref[...] = (numer * inv).astype(o_ref.dtype)
    lane = lax.broadcasted_iota(jnp.int32, (q.shape[0], 128), 1)
    stats = jnp.where(lane == 0, top, total)
    stat_ref[...] = stats.T[:8, :]


def attend(q, lens, rows, keys, dtype):
    n = q.shape[0]
    vmem = pl.BlockSpec(memory_space=pltpu.VMEM)
    return pl.pallas_call(
        attend_kernel,
        out_shape=(
            jax.ShapeDtypeStruct((n, LAT), dtype),
            jax.ShapeDtypeStruct((8, n), jnp.float32),
        ),
        in_specs=[vmem] * (3 + len(keys)),
        out_specs=(vmem, vmem),
        compiler_params=pltpu.CompilerParams(vmem_limit_bytes=32 * 1024 * 1024),
    )(q, lens, rows, *keys)


def on_device(latents, queries, hot_ids, lengths):
    group = lax.axis_index("ctx")
    rank = lax.axis_index("rep")
    by_column = latents.T
    owner = hot_ids // PER_DEV
    start = hot_ids % PER_DEV * BLK

    def piece(hop):
        at = (rank + hop) % N_REP * QUARTER
        return jnp.concatenate(
            [
                lax.dynamic_slice(by_column, (0, start[j] + at), (WIDTH, QUARTER))
                for j in range(HOT_GRP)
            ],
            axis=1,
        )

    arrived = {hop: shift_rep(piece(hop), hop) for hop in (2, 1, 3)}
    arrived[0] = piece(0)

    count = queries.shape[0]
    own = queries.reshape(count, -1, WIDTH).transpose(1, 0, 2).reshape(-1, WIDTH)
    along_z = jnp.concatenate([own] + [shift_z(own, hop) for hop in range(1, N_Z)], axis=0)
    asked = {hop: shift_x(along_z, hop) for hop in (2, 1, 3)}
    asked[0] = along_z
    hot_other = swap_core(hot_ids)

    slot = lax.broadcasted_iota(jnp.int32, (1, CHUNK), 1) // QUARTER
    source = jnp.where(slot == 0, owner[0], owner[1])
    mine = arrived[0]
    for hop in (1, 2, 3):
        mine = jnp.where(source == (rank - hop) % N_REP, arrived[hop], mine)
    here = {hop: shift_rep(mine, hop) for hop in (2, 1, 3)}
    here[0] = mine
    there = {hop: swap_core(here[hop]) for hop in (0, 1, 3, 2)}
    keys = [here[h] for h in range(N_REP)] + [there[h] for h in range(N_REP)]

    within = jnp.arange(CHUNK, dtype=jnp.int32) % QUARTER

    def rows_of(g, hot):
        base = jnp.where(slot[0] == 0, hot[0], hot[1])
        return jnp.concatenate(
            [
                (g * BPG + base) * BLK + (rank - hop) % N_REP * QUARTER + within
                for hop in range(N_REP)
            ]
        )

    rows = jnp.stack([rows_of(group, hot_ids), rows_of(group ^ 1, hot_other)])
    lens = jnp.tile(lengths, along_z.shape[0] // count)[:, None]

    parts = {}
    for hop in (2, 1, 3, 0):
        o, stat = attend(asked[hop], lens, rows, keys, jnp.bfloat16 if hop else jnp.float32)
        if hop:
            o, stat = shift_x(o, -hop), shift_x(stat, -hop)
        parts[hop] = (o, stat[0], stat[1])

    top = jnp.max(jnp.stack([p[1] for p in parts.values()]), axis=0)
    numer, total = 0.0, 0.0
    for o, m, t in parts.values():
        f = t * jnp.exp(m - top)
        numer = numer + o.astype(jnp.float32) * f[:, None]
        total = total + f

    n = own.shape[0]
    final = []
    for hop in (4, 3, 5, 2, 6, 1, 7, 0):
        cut = slice(hop * n, (hop + 1) * n)
        a, b = numer[cut], jnp.stack([top[cut], total[cut]])
        if hop:
            a, b = shift_z(a, -hop), shift_z(b, -hop)
        final.append((a, b[0], b[1]))
    top = jnp.max(jnp.stack([p[1] for p in final]), axis=0)
    numer, total = 0.0, 0.0
    for a, m, t in final:
        f = jnp.exp(m - top)
        numer = numer + a * f[:, None]
        total = total + t * f
    out = (numer / total[:, None]).astype(jnp.bfloat16)
    return out.reshape(-1, count, LAT).transpose(1, 0, 2).reshape(count, -1)


def solution(mesh):
    assert dict(mesh.shape) == {"ctx": N_X * N_Z * N_C, "rep": N_REP}
    placed = (P(("ctx", "rep"), None), P("rep", "ctx"), P("ctx"), P("rep"))
    return jax.shard_map(
        on_device, mesh=mesh, in_specs=placed, out_specs=P("rep", "ctx"), check_vma=False
    )
```

```python
import functools

import jax
import jax.numpy as jnp
from jax import lax
from jax.experimental import pallas as pl
from jax.experimental.pallas import tpu as pltpu
from jax.sharding import Mesh, PartitionSpec as P

H = 128
LAT = 512
ROPE = 64
QK = 192
BLK = 1024
HOT_GRP = 2
BPG = 16
WIDTH = LAT + ROPE
N_X = 4
N_Z = 8
N_C = 2
N_REP = 4
PER_DEV = BPG // N_REP
QUARTER = BLK // N_REP
HALF = QUARTER // 2
PAIR = HOT_GRP * HALF
CHUNK = 2 * PAIR
NEVER = -1e30
N_FAR = N_Z // 2
f32 = jnp.float32
bf16 = jnp.bfloat16

VMEM = pl.BlockSpec(memory_space=pltpu.VMEM)
SMEM = pl.BlockSpec(memory_space=pltpu.SMEM)
ANY = pl.BlockSpec(memory_space=pltpu.HBM)
PARAMS = pltpu.CompilerParams(vmem_limit_bytes=32 * 1024 * 1024)


def shift_rep(a, by):
    return lax.ppermute(a, "rep", [(i, (i + by) % N_REP) for i in range(N_REP)])


def swap_core(a):
    return lax.ppermute(a, "c", [(0, 1), (1, 0)])


def back_xz(a, hop, flip):
    pairs = []
    for x in range(N_X):
        for z in range(N_Z):
            pairs.append((x * N_Z + z, (x - hop) % N_X * N_Z + (z ^ flip)))
    return lax.ppermute(a, ("x", "z"), pairs)


def back_far(a, hop):
    pairs = [(z, (z - 2 * hop) % N_Z) for z in range(N_Z)]
    return lax.ppermute(a, "z", pairs)


def column(hot_ref, slot, rank, half):
    at = hot_ref[slot] % PER_DEV * BLK + rank * QUARTER + half * HALF
    return pl.ds(pl.multiple_of(at, HALF), HALF)


def run_copies(copies):
    for c in copies:
        c.start()
    for c in copies:
        c.wait()


def first_cut_kernel(hot_ref, lat_ref, up_ref, down_ref, sems):
    far = (lax.axis_index("rep") + 2) % N_REP
    copies = []
    for half, dst in enumerate((up_ref, down_ref)):
        for slot in range(HOT_GRP):
            copies.append(
                pltpu.make_async_copy(
                    lat_ref.at[:, column(hot_ref, slot, far, half)],
                    dst.at[:, pl.ds(slot * HALF, HALF)],
                    sems.at[len(copies)],
                )
            )
    run_copies(copies)


def own_cut_kernel(hot_ref, lat_ref, right_ref, left_ref, mine_ref, sems):
    rank = lax.axis_index("rep")
    copies = []
    for hop, dst in ((1, right_ref), (3, left_ref), (0, mine_ref)):
        for half in range(2):
            for slot in range(HOT_GRP):
                copies.append(
                    pltpu.make_async_copy(
                        lat_ref.at[:, column(hot_ref, slot, (rank + hop) % N_REP, half)],
                        dst.at[:, pl.ds(half * PAIR + slot * HALF, HALF)],
                        sems.at[len(copies)],
                    )
                )
    run_copies(copies)


def pass_on_kernel(hot_ref, from_left, from_right, right_in, left_in, right_ref, left_ref):
    rank = lax.axis_index("rep")
    for slot in range(HOT_GRP):
        a = slice(slot * HALF, (slot + 1) * HALF)
        b = slice(PAIR + slot * HALF, PAIR + (slot + 1) * HALF)

        @pl.when(hot_ref[slot] // PER_DEV != rank)
        def _():
            right_ref[:, a] = from_left[:, a]
            left_ref[:, b] = from_right[:, a]


def settle_kernel(hot_ref, from_left, from_right, mine_in, mine_ref):
    rank = lax.axis_index("rep")
    for slot in range(HOT_GRP):
        a = slice(slot * HALF, (slot + 1) * HALF)
        b = slice(PAIR + slot * HALF, PAIR + (slot + 1) * HALF)
        away = (hot_ref[slot] // PER_DEV - rank + N_REP) % N_REP

        @pl.when(away >= 2)
        def _():
            mine_ref[:, a] = from_left[:, a]

        @pl.when(away == 1)
        def _():
            mine_ref[:, a] = from_right[:, a]

        @pl.when(away == 3)
        def _():
            mine_ref[:, b] = from_left[:, b]

        @pl.when((away == 1) | (away == 2))
        def _():
            mine_ref[:, b] = from_right[:, b]


def three_terms(v):
    hi = v.astype(bf16)
    mid = (v - hi.astype(f32)).astype(bf16)
    low = (v - hi.astype(f32) - mid.astype(f32)).astype(bf16)
    return [hi, mid, low]


PLACES = ((0, 0, 2), (3, 0, 2), (1, 0, 2), (2, 0, 1), (2, 1, 1))


def attend_kernel(hop, q_ref, len_ref, hot_ref, hot_other_ref, *refs):
    n = len(PLACES)
    key_refs, outs = refs[: N_C * n], refs[N_C * n :]
    x, z, c = lax.axis_index("x"), lax.axis_index("z"), lax.axis_index("c")
    rank = lax.axis_index("rep")
    group = (x * N_Z + z) * N_C + c
    n_own = q_ref.shape[0] // (N_X * N_Z)
    first = (x - hop + N_X) % N_X * N_Z
    q = jnp.concatenate(
        [
            q_ref[
                pl.ds(pl.multiple_of((first + 2 * far + ((z + flip) & 1)) * n_own, n_own), n_own), :
            ]
            for flip in range(2)
            for far in range(N_FAR)
        ],
        axis=0,
    )
    lens = jnp.concatenate([len_ref[...]] * (q.shape[0] // len_ref.shape[0]), axis=0)
    lane = lax.broadcasted_iota(jnp.int32, (1, HALF), 1)
    parts = []
    for other in range(N_C):
        keys = key_refs[other * n : (other + 1) * n]
        hot = hot_other_ref if other else hot_ref
        own_group = group + other * (1 - 2 * c)
        scores = []
        for k_ref, (away, half, halves) in zip(keys, PLACES):
            at = (rank + away) % N_REP * QUARTER
            rows = jnp.concatenate(
                [
                    (own_group * BPG + hot[slot]) * BLK + at + h * HALF + lane
                    for h in range(half, half + halves)
                    for slot in range(HOT_GRP)
                ],
                axis=1,
            )
            s = jnp.dot(q, k_ref[...], preferred_element_type=f32) * (QK**-0.5)
            scores.append(jnp.where(rows < lens, s, NEVER))
        peak = scores[0].max(axis=1, keepdims=True)
        for s in scores[1:]:
            peak = jnp.maximum(peak, s.max(axis=1, keepdims=True))
        total = jnp.zeros_like(peak)
        numer = None
        for s, k_ref in zip(scores, keys):
            w = jnp.exp(s - peak).astype(bf16)
            total = total + jnp.sum(w.astype(f32), axis=1, keepdims=True)
            v = lax.dot_general(
                w, k_ref[:LAT, :], (((1,), (1,)), ((), ())), preferred_element_type=f32
            )
            numer = v if numer is None else numer + v
        parts.append((peak, total, numer))
    top = jnp.maximum(parts[0][0], parts[1][0])
    numer, total = 0.0, 0.0
    for peak, t, v in parts:
        f = jnp.where(peak > NEVER / 2, jnp.exp(peak - top), 0.0)
        numer = numer + v * f
        total = total + t * f
    o = (numer * (1.0 / jnp.maximum(total, 1.0))).astype(bf16)
    lanes = lax.broadcasted_iota(jnp.int32, (q.shape[0], 128), 1)
    stats = jnp.where(lanes == 0, top, total).T[:2, :]
    rows = o.shape[0] // 2
    for flip, o_ref in enumerate(outs):
        o_ref[:rows, :] = o[flip * rows : (flip + 1) * rows]
        mine = stats[:, flip * rows : (flip + 1) * rows]
        terms = three_terms(mine[0:1]) + three_terms(mine[1:2])
        terms = [t.astype(f32) for t in terms] + [jnp.zeros((10, rows), f32)]
        o_ref[rows:, :rows] = jnp.concatenate(terms, axis=0).astype(bf16)
        o_ref[rows:, rows:] = jnp.zeros((16, LAT - rows), bf16)


def merge_kernel(*refs):
    n_in = N_X * 2
    parts, sends, (own_ref, stat_ref), (acc_ref,) = (
        refs[:n_in],
        refs[n_in : n_in + N_FAR - 1],
        refs[n_in + N_FAR - 1 : n_in + N_FAR + 1],
        refs[n_in + N_FAR + 1 :],
    )
    rows = parts[0].shape[0] - 16
    tops, totals = [], []
    for p in parts:
        s = p[rows:, :rows].astype(f32)
        tops.append(s[0:1] + s[1:2] + s[2:3])
        totals.append(s[3:4] + s[4:5] + s[5:6])
    top = functools.reduce(jnp.maximum, tops)
    weights = [t * jnp.exp(m - top) for m, t in zip(tops, totals)]
    total = sum(weights)
    inv = 1.0 / jnp.maximum(total, 1.0)
    table = [w * inv for w in weights] + [top, total]
    table.append(jnp.zeros((128 - len(table), rows), f32))
    table = jnp.concatenate(table, axis=0).T
    acc = 0.0
    for i, p in enumerate(parts):
        acc = acc + p[:rows, :].astype(f32) * table[:, i : i + 1]
    acc_ref[:, :LAT] = acc
    acc_ref[:, LAT:] = table
    far = lax.axis_index("z") // 2
    n = rows // N_FAR

    def block(hop):
        return acc_ref[pl.ds(pl.multiple_of((far - hop + N_FAR) % N_FAR * n, n), n), :]

    lane = lax.broadcasted_iota(jnp.int32, (n, 128), 1)
    for hop, ref in enumerate(sends, 1):
        b = block(hop)
        ref[:, :LAT] = b[:, :LAT].astype(bf16)
        top, total = b[:, LAT + n_in : LAT + n_in + 1], b[:, LAT + n_in + 1 : LAT + n_in + 2]
        packed = jnp.zeros((n, 128), f32)
        for i, term in enumerate(three_terms(top) + three_terms(total)):
            packed = jnp.where(lane == i, term.astype(f32), packed)
        ref[:, LAT:] = packed.astype(bf16)
    b = block(0)
    own_ref[...] = b[:, :LAT]
    stat_ref[...] = b[:, LAT:]


def finish_kernel(own_ref, stat_ref, *refs):
    parts, out_ref = refs[:-1], refs[-1]
    n_in = N_X * 2
    tops, totals, values = [stat_ref[:, n_in : n_in + 1]], [stat_ref[:, n_in + 1 : n_in + 2]], [own_ref[...]]
    for p in parts:
        s = p[:, LAT:].astype(f32)
        tops.append(s[:, 0:1] + s[:, 1:2] + s[:, 2:3])
        totals.append(s[:, 3:4] + s[:, 4:5] + s[:, 5:6])
        values.append(p[:, :LAT].astype(f32))
    top = functools.reduce(jnp.maximum, tops)
    weights = [t * jnp.exp(m - top) for m, t in zip(tops, totals)]
    total = sum(weights)
    o = sum(v * w for v, w in zip(values, weights)) / total
    count = out_ref.shape[0]
    for head in range(o.shape[0] // count):
        out_ref[:, head * LAT : (head + 1) * LAT] = o[head * count : (head + 1) * count].astype(bf16)


def call(kernel, outs, in_specs, args, **more):
    return pl.pallas_call(
        kernel,
        out_shape=tuple(jax.ShapeDtypeStruct(*o) for o in outs),
        in_specs=in_specs,
        out_specs=(VMEM,) * len(outs),
        compiler_params=PARAMS,
        **more,
    )(*args)


def on_device(latents, queries, hot_ids, lengths):
    by_column = latents.T
    count = queries.shape[0]
    chunk, pair = ((WIDTH, CHUNK), bf16), ((WIDTH, PAIR), bf16)

    up, down = call(
        first_cut_kernel,
        [pair, pair],
        [SMEM, ANY],
        [hot_ids, by_column],
        scratch_shapes=[pltpu.SemaphoreType.DMA((4,))],
    )
    up, down = shift_rep(up, 1), shift_rep(down, -1)
    right, left, mine = call(
        own_cut_kernel,
        [chunk] * 3,
        [SMEM, ANY],
        [hot_ids, by_column],
        scratch_shapes=[pltpu.SemaphoreType.DMA((12,))],
    )
    right, left = call(
        pass_on_kernel,
        [chunk] * 2,
        [SMEM] + [VMEM] * 4,
        [hot_ids, up, down, right, left],
        input_output_aliases={3: 0, 4: 1},
    )
    from_left, from_right = shift_rep(right, 1), shift_rep(left, -1)
    (mine,) = call(
        settle_kernel,
        [chunk],
        [SMEM] + [VMEM] * 3,
        [hot_ids, from_left, from_right, mine],
        input_output_aliases={3: 0},
    )

    own = queries.reshape(count, -1, WIDTH).transpose(1, 0, 2).reshape(-1, WIDTH)
    asked = lax.all_gather(own, "z", tiled=True)
    asked = lax.all_gather(asked, "x", tiled=True)
    hot_other = swap_core(hot_ids)

    of_left, of_right = shift_rep(mine, 1), shift_rep(mine, -1)
    far_a, far_b = shift_rep(of_left[:, :PAIR], 1), shift_rep(of_right[:, PAIR:], -1)
    keys = [mine, of_left, of_right, far_a, far_b]
    keys = keys + [swap_core(k) for k in keys]

    rows = asked.shape[0] // N_X // 2
    part = ((rows + 16, LAT), bf16)
    lens = lengths[:, None]
    parts = []
    for hop in (2, 1, 3, 0):
        same, flipped = call(
            functools.partial(attend_kernel, hop),
            [part, part],
            [VMEM, VMEM, SMEM, SMEM] + [VMEM] * len(keys),
            [asked, lens, hot_ids, hot_other] + keys,
        )
        parts.append(back_xz(flipped, hop, 1))
        parts.append(back_xz(same, hop, 0) if hop else same)

    n = own.shape[0]
    message = ((n, LAT + 128), bf16)
    *sends, mine, stat = call(
        merge_kernel,
        [message] * (N_FAR - 1) + [((n, LAT), f32), ((n, 128), f32)],
        [VMEM] * len(parts),
        parts,
        scratch_shapes=[pltpu.VMEM((rows, LAT + 128), f32)],
    )
    sends = [back_far(s, hop) for hop, s in enumerate(sends, 1)]
    (out,) = call(
        finish_kernel,
        [((count, n // count * LAT), bf16)],
        [VMEM] * (2 + len(sends)),
        [mine, stat, *sends],
    )
    return out


def solution(mesh):
    assert dict(mesh.shape) == {"ctx": N_X * N_Z * N_C, "rep": N_REP}
    split = Mesh(mesh.devices.reshape(N_X, N_Z, N_C, N_REP), ("x", "z", "c", "rep"))
    ctx = ("x", "z", "c")
    placed = (P((*ctx, "rep"), None), P("rep", ctx), P(ctx), P("rep"))
    return jax.shard_map(
        on_device, mesh=split, in_specs=placed, out_specs=P("rep", ctx), check_vma=False
    )
```

```python
import functools

import jax
import jax.numpy as jnp
from jax import lax
from jax.experimental import pallas as pl
from jax.experimental.pallas import tpu as pltpu
from jax.sharding import Mesh, PartitionSpec as P

H = 128
LAT = 512
ROPE = 64
QK = 192
BLK = 1024
HOT_GRP = 2
BPG = 16
WIDTH = LAT + ROPE
N_X = 4
N_Z = 8
N_C = 2
N_REP = 4
PER_DEV = BPG // N_REP
QUARTER = BLK // N_REP
HALF = QUARTER // 2
PAIR = HOT_GRP * HALF
CHUNK = 2 * PAIR
NEVER = -1e30
SCALE = QK**-0.5
LOG2_E = 1.4426950408889634
N_FAR = N_Z // 2
f32 = jnp.float32
bf16 = jnp.bfloat16

VMEM = pl.BlockSpec(memory_space=pltpu.VMEM)
SMEM = pl.BlockSpec(memory_space=pltpu.SMEM)
ANY = pl.BlockSpec(memory_space=pltpu.HBM)
MIB = 1024 * 1024


def shift_rep(a, by):
    return lax.ppermute(a, "rep", [(i, (i + by) % N_REP) for i in range(N_REP)])


def swap_core(a):
    return lax.ppermute(a, "c", [(0, 1), (1, 0)])


def cross_x(a, bits):
    return lax.ppermute(a, "x", [(i, i ^ bits) for i in range(N_X)])


def cross_z(a, bits):
    return lax.ppermute(a, "z", [(i, i ^ bits) for i in range(N_Z)])


def cross_xz(a, bits_x, bits_z):
    pairs = []
    for x in range(N_X):
        for z in range(N_Z):
            pairs.append((x * N_Z + z, (x ^ bits_x) * N_Z + (z ^ bits_z)))
    return lax.ppermute(a, ("x", "z"), pairs)


def column(hot_ref, slot, rank, half):
    at = hot_ref[slot] % PER_DEV * BLK + rank * QUARTER + half * HALF
    return pl.ds(pl.multiple_of(at, HALF), HALF)


def run_copies(copies):
    for c in copies:
        c.start()
    for c in copies:
        c.wait()


def first_cut_kernel(hot_ref, lat_ref, up_ref, down_ref, sems):
    far = (lax.axis_index("rep") + 2) % N_REP
    copies = []
    for half, dst in enumerate((up_ref, down_ref)):
        for slot in range(HOT_GRP):
            copies.append(
                pltpu.make_async_copy(
                    lat_ref.at[:, column(hot_ref, slot, far, half)],
                    dst.at[:, pl.ds(slot * HALF, HALF)],
                    sems.at[len(copies)],
                )
            )
    run_copies(copies)


def own_cut_kernel(hot_ref, lat_ref, right_ref, left_ref, mine_ref, sems):
    rank = lax.axis_index("rep")
    copies = []
    for hop, dst in ((1, right_ref), (3, left_ref), (0, mine_ref)):
        for half in range(2):
            for slot in range(HOT_GRP):
                copies.append(
                    pltpu.make_async_copy(
                        lat_ref.at[:, column(hot_ref, slot, (rank + hop) % N_REP, half)],
                        dst.at[:, pl.ds(half * PAIR + slot * HALF, HALF)],
                        sems.at[len(copies)],
                    )
                )
    run_copies(copies)


def pass_on_kernel(hot_ref, from_left, from_right, right_in, left_in, right_ref, left_ref):
    rank = lax.axis_index("rep")
    right_ref[:, PAIR:] = right_in[:, PAIR:]
    left_ref[:, :PAIR] = left_in[:, :PAIR]
    for slot in range(HOT_GRP):
        a = slice(slot * HALF, (slot + 1) * HALF)
        b = slice(PAIR + slot * HALF, PAIR + (slot + 1) * HALF)
        here = hot_ref[slot] // PER_DEV == rank

        @pl.when(here)
        def _():
            right_ref[:, a] = right_in[:, a]
            left_ref[:, b] = left_in[:, b]

        @pl.when(jnp.logical_not(here))
        def _():
            right_ref[:, a] = from_left[:, a]
            left_ref[:, b] = from_right[:, a]


def settle_kernel(hot_ref, from_left, from_right, mine_in, mine_ref):
    rank = lax.axis_index("rep")
    for slot in range(HOT_GRP):
        a = slice(slot * HALF, (slot + 1) * HALF)
        b = slice(PAIR + slot * HALF, PAIR + (slot + 1) * HALF)
        away = (hot_ref[slot] // PER_DEV - rank + N_REP) % N_REP

        @pl.when(away == 0)
        def _():
            mine_ref[:, a] = mine_in[:, a]
            mine_ref[:, b] = mine_in[:, b]

        @pl.when(away >= 2)
        def _():
            mine_ref[:, a] = from_left[:, a]

        @pl.when(away == 1)
        def _():
            mine_ref[:, a] = from_right[:, a]

        @pl.when(away == 3)
        def _():
            mine_ref[:, b] = from_left[:, b]

        @pl.when((away == 1) | (away == 2))
        def _():
            mine_ref[:, b] = from_right[:, b]


def three_terms(v):
    hi = v.astype(bf16)
    mid = (v - hi.astype(f32)).astype(bf16)
    low = (v - hi.astype(f32) - mid.astype(f32)).astype(bf16)
    return [hi, mid, low]


PLACES = ((0, 0, 2), (3, 0, 2), (1, 0, 2), (2, 0, 1), (2, 1, 1))


def attend_kernel(q_ref, len_ref, hot_ref, hot_other_ref, *refs):
    n = len(PLACES)
    key_refs, outs = refs[: N_C * n], refs[N_C * n :]
    x, z, c = lax.axis_index("x"), lax.axis_index("z"), lax.axis_index("c")
    rank = lax.axis_index("rep")
    group = (x * N_Z + z) * N_C + c
    q = q_ref[...]
    count = len_ref.shape[0]
    line = lax.broadcasted_iota(jnp.int32, (count, 1), 0)
    lens = jnp.zeros((count, 1), jnp.int32)
    for i in range(count):
        lens = jnp.where(line == i, len_ref[i], lens)
    lens = jnp.concatenate([lens] * (q.shape[0] // count), axis=0)
    lane = lax.broadcasted_iota(jnp.int32, (1, HALF), 1)
    parts = []
    for other in range(N_C):
        keys = key_refs[other * n : (other + 1) * n]
        hot = hot_other_ref if other else hot_ref
        own_group = group + other * (1 - 2 * c)
        scores = []
        for k_ref, (away, half, halves) in zip(keys, PLACES):
            at = (rank + away) % N_REP * QUARTER
            rows = jnp.concatenate(
                [
                    (own_group * BPG + hot[slot]) * BLK + at + h * HALF + lane
                    for h in range(half, half + halves)
                    for slot in range(HOT_GRP)
                ],
                axis=1,
            )
            s = jnp.dot(q, k_ref[...], preferred_element_type=f32)
            scores.append(jnp.where(rows < lens, s, NEVER))
        peak = scores[0].max(axis=1, keepdims=True)
        for s in scores[1:]:
            peak = jnp.maximum(peak, s.max(axis=1, keepdims=True))
        total = jnp.zeros_like(peak)
        numer = None
        for s, k_ref in zip(scores, keys):
            w = jnp.exp2((s - peak) * (SCALE * LOG2_E)).astype(bf16)
            total = total + jnp.sum(w.astype(f32), axis=1, keepdims=True)
            v = lax.dot_general(
                w, k_ref[:LAT, :], (((1,), (1,)), ((), ())), preferred_element_type=f32
            )
            numer = v if numer is None else numer + v
        parts.append((peak, total, numer))
    top = jnp.maximum(parts[0][0], parts[1][0])
    numer, total = 0.0, 0.0
    for peak, t, v in parts:
        f = jnp.where(peak > NEVER / 2, jnp.exp((peak - top) * SCALE), 0.0)
        numer = numer + v * f
        total = total + t * f
    o = (numer * (1.0 / jnp.maximum(total, 1.0))).astype(bf16)
    lanes = lax.broadcasted_iota(jnp.int32, (q.shape[0], 128), 1)
    stats = jnp.where(lanes == 0, top * SCALE, total).T[:2, :]
    rows = o.shape[0] // 2
    for flip, o_ref in enumerate(outs):
        o_ref[:rows, :] = o[flip * rows : (flip + 1) * rows]
        mine = stats[:, flip * rows : (flip + 1) * rows]
        terms = three_terms(mine[0:1]) + three_terms(mine[1:2])
        terms = [t.astype(f32) for t in terms] + [jnp.zeros((10, rows), f32)]
        o_ref[rows:, :rows] = jnp.concatenate(terms, axis=0).astype(bf16)
        o_ref[rows:, rows:] = jnp.zeros((16, LAT - rows), bf16)


def merge_kernel(*refs):
    n_in = N_X * 2
    parts, sends, (own_ref, stat_ref) = (
        refs[:n_in],
        refs[n_in : n_in + N_FAR - 1],
        refs[n_in + N_FAR - 1 :],
    )
    rows = parts[0].shape[0] - 16
    tops, totals = [], []
    for p in parts:
        s = p[rows:, :rows].astype(f32)
        tops.append(s[0:1] + s[1:2] + s[2:3])
        totals.append(s[3:4] + s[4:5] + s[5:6])
    top = functools.reduce(jnp.maximum, tops)
    weights = [t * jnp.exp(m - top) for m, t in zip(tops, totals)]
    total = sum(weights)
    inv = 1.0 / jnp.maximum(total, 1.0)
    table = [w * inv for w in weights] + [top, total]
    table.append(jnp.zeros((128 - len(table), rows), f32))
    table = jnp.concatenate(table, axis=0).T
    n = rows // N_FAR
    lane = lax.broadcasted_iota(jnp.int32, (n, 128), 1)
    for far in range(N_FAR):
        at = slice(far * n, (far + 1) * n)
        acc = 0.0
        for i, p in enumerate(parts):
            acc = acc + p[at, :].astype(f32) * table[at, i : i + 1]
        if far:
            ref = sends[far - 1]
            ref[:, :LAT] = acc.astype(bf16)
            packed = jnp.zeros((n, 128), f32)
            terms = three_terms(table[at, n_in : n_in + 1])
            terms += three_terms(table[at, n_in + 1 : n_in + 2])
            for i, term in enumerate(terms):
                packed = jnp.where(lane == i, term.astype(f32), packed)
            ref[:, LAT:] = packed.astype(bf16)
        else:
            own_ref[...] = acc
            stat_ref[...] = table[at]


def finish_kernel(own_ref, stat_ref, *refs):
    parts, out_ref = refs[:-1], refs[-1]
    n_in = N_X * 2
    tops, totals, values = [stat_ref[:, n_in : n_in + 1]], [stat_ref[:, n_in + 1 : n_in + 2]], [own_ref[...]]
    for p in parts:
        s = p[:, LAT:].astype(f32)
        tops.append(s[:, 0:1] + s[:, 1:2] + s[:, 2:3])
        totals.append(s[:, 3:4] + s[:, 4:5] + s[:, 5:6])
        values.append(p[:, :LAT].astype(f32))
    top = functools.reduce(jnp.maximum, tops)
    weights = [t * jnp.exp(m - top) for m, t in zip(tops, totals)]
    total = sum(weights)
    o = sum(v * w for v, w in zip(values, weights)) / total
    count = out_ref.shape[0]
    for head in range(o.shape[0] // count):
        out_ref[:, head * LAT : (head + 1) * LAT] = o[head * count : (head + 1) * count].astype(bf16)


def call(kernel, outs, in_specs, args, mib=16, **more):
    return pl.pallas_call(
        kernel,
        out_shape=tuple(jax.ShapeDtypeStruct(*o) for o in outs),
        in_specs=in_specs,
        out_specs=(VMEM,) * len(outs),
        compiler_params=pltpu.CompilerParams(vmem_limit_bytes=mib * MIB),
        **more,
    )(*args)


def on_device(latents, queries, hot_ids, lengths):
    by_column = latents.T
    count = queries.shape[0]
    chunk, pair = ((WIDTH, CHUNK), bf16), ((WIDTH, PAIR), bf16)

    up, down = call(
        first_cut_kernel,
        [pair, pair],
        [SMEM, ANY],
        [hot_ids, by_column],
        mib=50,
        scratch_shapes=[pltpu.SemaphoreType.DMA((4,))],
    )
    up, down = shift_rep(up, 1), shift_rep(down, -1)
    right, left, mine = call(
        own_cut_kernel,
        [chunk] * 3,
        [SMEM, ANY],
        [hot_ids, by_column],
        mib=50,
        scratch_shapes=[pltpu.SemaphoreType.DMA((12,))],
    )
    right, left = call(
        pass_on_kernel,
        [chunk] * 2,
        [SMEM] + [VMEM] * 4,
        [hot_ids, up, down, right, left],
    )
    from_left, from_right = shift_rep(right, 1), shift_rep(left, -1)
    (mine,) = call(
        settle_kernel,
        [chunk],
        [SMEM] + [VMEM] * 3,
        [hot_ids, from_left, from_right, mine],
    )

    own = queries.reshape(count, -1, WIDTH).transpose(1, 0, 2).reshape(-1, WIDTH)
    near = own
    for bits in (2, 4, 1):
        near = jnp.concatenate([near, cross_z(near, bits)], axis=0)
    asked = [near] + [cross_x(near, bits) for bits in range(1, N_X)]
    hot_other = swap_core(hot_ids)

    of_left, of_right = shift_rep(mine, 1), shift_rep(mine, -1)
    far_a, far_b = shift_rep(of_left[:, :PAIR], 1), shift_rep(of_right[:, PAIR:], -1)
    keys = [mine, of_left, of_right, far_a, far_b]
    keys = keys + [swap_core(k) for k in keys]

    rows = near.shape[0] // 2
    part = ((rows + 16, LAT), bf16)
    parts = []
    for hop in (2, 1, 3, 0):
        same, flipped = call(
            attend_kernel,
            [part, part],
            [VMEM, SMEM, SMEM, SMEM] + [VMEM] * len(keys),
            [asked[hop], lengths, hot_ids, hot_other] + keys,
        )
        lengths, same, flipped = lax.optimization_barrier((lengths, same, flipped))
        parts.append(cross_xz(flipped, hop, 1))
        parts.append(cross_xz(same, hop, 0) if hop else same)

    n = own.shape[0]
    message = ((n, LAT + 128), bf16)
    *sends, mine, stat = call(
        merge_kernel,
        [message] * (N_FAR - 1) + [((n, LAT), f32), ((n, 128), f32)],
        [VMEM] * len(parts),
        parts,
    )
    sends = [cross_z(s, 2 * far) for far, s in enumerate(sends, 1)]
    (out,) = call(
        finish_kernel,
        [((count, n // count * LAT), bf16)],
        [VMEM] * (2 + len(sends)),
        [mine, stat, *sends],
    )
    return out


def solution(mesh):
    assert dict(mesh.shape) == {"ctx": N_X * N_Z * N_C, "rep": N_REP}
    split = Mesh(mesh.devices.reshape(N_X, N_Z, N_C, N_REP), ("x", "z", "c", "rep"))
    ctx = ("x", "z", "c")
    placed = (P((*ctx, "rep"), None), P("rep", ctx), P(ctx), P("rep"))
    return jax.shard_map(
        on_device, mesh=split, in_specs=placed, out_specs=P("rep", ctx), check_vma=False
    )
```

```python
import functools

import jax
import jax.numpy as jnp
from jax import lax
from jax.experimental import pallas as pl
from jax.experimental.pallas import tpu as pltpu
from jax.sharding import Mesh, PartitionSpec as P

H = 128
LAT = 512
ROPE = 64
QK = 192
BLK = 1024
HOT_GRP = 2
BPG = 16
WIDTH = LAT + ROPE
N_X = 4
N_Z = 8
N_C = 2
N_REP = 4
PER_DEV = BPG // N_REP
QUARTER = BLK // N_REP
HALF = QUARTER // 2
PAIR = HOT_GRP * HALF
CHUNK = 2 * PAIR
NEVER = -1e30
STAT_ROWS = 8
SCALE = QK**-0.5
LOG2_E = 1.4426950408889634
N_FAR = N_Z // 2
f32 = jnp.float32
bf16 = jnp.bfloat16

VMEM = pl.BlockSpec(memory_space=pltpu.VMEM)
SMEM = pl.BlockSpec(memory_space=pltpu.SMEM)
ANY = pl.BlockSpec(memory_space=pltpu.HBM)
MIB = 1024 * 1024


def shift_rep(a, by):
    return lax.ppermute(a, "rep", [(i, (i + by) % N_REP) for i in range(N_REP)])


def swap_core(a):
    return lax.ppermute(a, "c", [(0, 1), (1, 0)])


def cross_x(a, bits):
    return lax.ppermute(a, "x", [(i, i ^ bits) for i in range(N_X)])


def cross_z(a, bits):
    return lax.ppermute(a, "z", [(i, i ^ bits) for i in range(N_Z)])


def cross_xz(a, bits_x, bits_z):
    pairs = []
    for x in range(N_X):
        for z in range(N_Z):
            pairs.append((x * N_Z + z, (x ^ bits_x) * N_Z + (z ^ bits_z)))
    return lax.ppermute(a, ("x", "z"), pairs)


def column(hot_ref, slot, rank, half):
    at = hot_ref[slot] % PER_DEV * BLK + rank * QUARTER + half * HALF
    return pl.ds(pl.multiple_of(at, HALF), HALF)


def run_copies(copies):
    for c in copies:
        c.start()
    for c in copies:
        c.wait()


def first_cut_kernel(hot_ref, lat_ref, up_ref, down_ref, sems):
    far = (lax.axis_index("rep") + 2) % N_REP
    copies = []
    for half, dst in enumerate((up_ref, down_ref)):
        for slot in range(HOT_GRP):
            copies.append(
                pltpu.make_async_copy(
                    lat_ref.at[:, column(hot_ref, slot, far, half)],
                    dst.at[:, pl.ds(slot * HALF, HALF)],
                    sems.at[len(copies)],
                )
            )
    run_copies(copies)


def own_cut_kernel(hot_ref, lat_ref, right_ref, left_ref, mine_ref, sems):
    rank = lax.axis_index("rep")
    copies = []
    for hop, dst in ((1, right_ref), (3, left_ref), (0, mine_ref)):
        for half in range(2):
            for slot in range(HOT_GRP):
                copies.append(
                    pltpu.make_async_copy(
                        lat_ref.at[:, column(hot_ref, slot, (rank + hop) % N_REP, half)],
                        dst.at[:, pl.ds(half * PAIR + slot * HALF, HALF)],
                        sems.at[len(copies)],
                    )
                )
    run_copies(copies)


def pass_on_kernel(hot_ref, from_left, from_right, right_in, left_in, right_ref, left_ref):
    rank = lax.axis_index("rep")
    right_ref[:, PAIR:] = right_in[:, PAIR:]
    left_ref[:, :PAIR] = left_in[:, :PAIR]
    for slot in range(HOT_GRP):
        a = slice(slot * HALF, (slot + 1) * HALF)
        b = slice(PAIR + slot * HALF, PAIR + (slot + 1) * HALF)
        here = hot_ref[slot] // PER_DEV == rank

        @pl.when(here)
        def _():
            right_ref[:, a] = right_in[:, a]
            left_ref[:, b] = left_in[:, b]

        @pl.when(jnp.logical_not(here))
        def _():
            right_ref[:, a] = from_left[:, a]
            left_ref[:, b] = from_right[:, a]


def settle_kernel(hot_ref, from_left, from_right, mine_in, mine_ref):
    rank = lax.axis_index("rep")
    for slot in range(HOT_GRP):
        a = slice(slot * HALF, (slot + 1) * HALF)
        b = slice(PAIR + slot * HALF, PAIR + (slot + 1) * HALF)
        away = (hot_ref[slot] // PER_DEV - rank + N_REP) % N_REP

        @pl.when(away == 0)
        def _():
            mine_ref[:, a] = mine_in[:, a]
            mine_ref[:, b] = mine_in[:, b]

        @pl.when(away >= 2)
        def _():
            mine_ref[:, a] = from_left[:, a]

        @pl.when(away == 1)
        def _():
            mine_ref[:, a] = from_right[:, a]

        @pl.when(away == 3)
        def _():
            mine_ref[:, b] = from_left[:, b]

        @pl.when((away == 1) | (away == 2))
        def _():
            mine_ref[:, b] = from_right[:, b]


def three_terms(v):
    hi = v.astype(bf16)
    mid = (v - hi.astype(f32)).astype(bf16)
    low = (v - hi.astype(f32) - mid.astype(f32)).astype(bf16)
    return [hi, mid, low]


def visible_lengths(len_ref, rows):
    count = len_ref.shape[0]
    line = lax.broadcasted_iota(jnp.int32, (count, 1), 0)
    lens = jnp.zeros((count, 1), jnp.int32)
    for i in range(count):
        lens = jnp.where(line == i, len_ref[i], lens)
    return jnp.concatenate([lens] * (rows // count), axis=0)


def row_numbers(hot_ref, other, away, half, halves):
    x, z, c = lax.axis_index("x"), lax.axis_index("z"), lax.axis_index("c")
    group = (x * N_Z + z) * N_C + c + other * (1 - 2 * c)
    at = (lax.axis_index("rep") + away) % N_REP * QUARTER
    lane = lax.broadcasted_iota(jnp.int32, (1, HALF), 1)
    return jnp.concatenate(
        [
            (group * BPG + hot_ref[slot]) * BLK + at + h * HALF + lane
            for h in range(half, half + halves)
            for slot in range(HOT_GRP)
        ],
        axis=1,
    )


NEAR = (0, 3, 1)
FAR = 2


def fold(op, s):
    return functools.reduce(op, [s[:, i : i + 128] for i in range(0, s.shape[1], 128)])


def score_kernel(other, len_ref, hot_ref, *refs):
    q_refs, key_refs, outs = refs[:N_X], refs[N_X : N_X + len(NEAR)], refs[N_X + len(NEAR) :]
    lens = visible_lengths(len_ref, q_refs[0].shape[0])
    rows = [row_numbers(hot_ref, other, away, 0, 2) for away in NEAR]
    for i, q_ref in enumerate(q_refs):
        s_ref, peak_ref = outs[2 * i : 2 * i + 2]
        q = q_ref[...]
        peaks = []
        for j, k_ref in enumerate(key_refs):
            s = jnp.dot(q, k_ref[...], preferred_element_type=f32)
            s = jnp.where(rows[j] < lens, s, NEVER)
            s_ref[:, j * CHUNK : (j + 1) * CHUNK] = s
            peaks.append(fold(jnp.maximum, s))
        peak_ref[...] = functools.reduce(jnp.maximum, peaks)


def attend_kernel(q_ref, *refs):
    n = len(NEAR)
    (s_refs, peak_refs), refs = (refs[0:4:2], refs[1:4:2]), refs[4:]
    (len_ref, *hot_refs), refs = refs[:3], refs[3:]
    key_refs, outs = refs[: N_C * (n + 2)], refs[N_C * (n + 2) :]
    q = q_ref[...]
    lens = visible_lengths(len_ref, q.shape[0])
    last = []
    for other in range(N_C):
        for half in range(2):
            k_ref = key_refs[other * (n + 2) + n + half]
            rows = row_numbers(hot_refs[other], other, FAR, half, 1)
            s = jnp.dot(q, k_ref[...], preferred_element_type=f32)
            last.append(jnp.where(rows < lens, s, NEVER))
    parts = []
    for other in range(N_C):
        keys = key_refs[other * (n + 2) : (other + 1) * (n + 2)]
        scores = [s_refs[other][:, i * CHUNK : (i + 1) * CHUNK] for i in range(n)]
        scores += last[other * 2 : other * 2 + 2]
        peak = peak_refs[other][...]
        for s in last[other * 2 : other * 2 + 2]:
            peak = jnp.maximum(peak, fold(jnp.maximum, s))
        peak = peak.max(axis=1, keepdims=True)
        total = 0.0
        numer = None
        for s, k_ref in zip(scores, keys):
            w = jnp.exp2((s - peak) * (SCALE * LOG2_E)).astype(bf16)
            total = total + fold(jnp.add, w.astype(f32))
            v = lax.dot_general(
                w, k_ref[:LAT, :], (((1,), (1,)), ((), ())), preferred_element_type=f32
            )
            numer = v if numer is None else numer + v
        parts.append((peak, total.sum(axis=1, keepdims=True), numer))
    top = jnp.maximum(parts[0][0], parts[1][0])
    numer, total = 0.0, 0.0
    for peak, t, v in parts:
        f = jnp.where(peak > NEVER / 2, jnp.exp((peak - top) * SCALE), 0.0)
        numer = numer + v * f
        total = total + t * f
    o = (numer * (1.0 / jnp.maximum(total, 1.0))).astype(bf16)
    lanes = lax.broadcasted_iota(jnp.int32, (q.shape[0], 128), 1)
    stats = jnp.where(lanes == 0, top * SCALE, total).T[:2, :]
    rows = o.shape[0] // 2
    for flip, o_ref in enumerate(outs):
        o_ref[:rows, :] = o[flip * rows : (flip + 1) * rows]
        mine = stats[:, flip * rows : (flip + 1) * rows]
        terms = three_terms(mine[0:1]) + three_terms(mine[1:2])
        terms = [t.astype(f32) for t in terms] + [jnp.zeros((STAT_ROWS - 6, rows), f32)]
        o_ref[rows:, :rows] = jnp.concatenate(terms, axis=0).astype(bf16)
        o_ref[rows:, rows:] = jnp.zeros((STAT_ROWS, LAT - rows), bf16)


def merge_kernel(*refs):
    n_in = N_X * 2
    parts, sends, (own_ref, stat_ref) = (
        refs[:n_in],
        refs[n_in : n_in + N_FAR - 1],
        refs[n_in + N_FAR - 1 :],
    )
    rows = parts[0].shape[0] - STAT_ROWS
    tops, totals = [], []
    for p in parts:
        s = p[rows:, :rows].astype(f32)
        tops.append(s[0:1] + s[1:2] + s[2:3])
        totals.append(s[3:4] + s[4:5] + s[5:6])
    top = functools.reduce(jnp.maximum, tops)
    weights = [t * jnp.exp(m - top) for m, t in zip(tops, totals)]
    total = sum(weights)
    inv = 1.0 / jnp.maximum(total, 1.0)
    table = [w * inv for w in weights] + [top, total]
    table.append(jnp.zeros((128 - len(table), rows), f32))
    table = jnp.concatenate(table, axis=0).T
    n = rows // N_FAR
    lane = lax.broadcasted_iota(jnp.int32, (n, 128), 1)
    for far in range(N_FAR):
        at = slice(far * n, (far + 1) * n)
        acc = 0.0
        for i, p in enumerate(parts):
            acc = acc + p[at, :].astype(f32) * table[at, i : i + 1]
        if far:
            ref = sends[far - 1]
            ref[:, :LAT] = acc.astype(bf16)
            packed = jnp.zeros((n, 128), f32)
            terms = three_terms(table[at, n_in : n_in + 1])
            terms += three_terms(table[at, n_in + 1 : n_in + 2])
            for i, term in enumerate(terms):
                packed = jnp.where(lane == i, term.astype(f32), packed)
            ref[:, LAT:] = packed.astype(bf16)
        else:
            own_ref[...] = acc
            stat_ref[...] = table[at]


def finish_kernel(own_ref, stat_ref, *refs):
    parts, out_ref = refs[:-1], refs[-1]
    n_in = N_X * 2
    tops, totals, values = [stat_ref[:, n_in : n_in + 1]], [stat_ref[:, n_in + 1 : n_in + 2]], [own_ref[...]]
    for p in parts:
        s = p[:, LAT:].astype(f32)
        tops.append(s[:, 0:1] + s[:, 1:2] + s[:, 2:3])
        totals.append(s[:, 3:4] + s[:, 4:5] + s[:, 5:6])
        values.append(p[:, :LAT].astype(f32))
    top = functools.reduce(jnp.maximum, tops)
    weights = [t * jnp.exp(m - top) for m, t in zip(tops, totals)]
    total = sum(weights)
    o = sum(v * w for v, w in zip(values, weights)) / total
    count = out_ref.shape[0]
    for head in range(o.shape[0] // count):
        out_ref[:, head * LAT : (head + 1) * LAT] = o[head * count : (head + 1) * count].astype(bf16)


def call(kernel, outs, in_specs, args, mib=16, flops=0, **more):
    if flops:
        more["cost_estimate"] = pl.CostEstimate(
            flops=flops, bytes_accessed=8 * MIB, transcendentals=0
        )
    return pl.pallas_call(
        kernel,
        out_shape=tuple(jax.ShapeDtypeStruct(*o) for o in outs),
        in_specs=in_specs,
        out_specs=(VMEM,) * len(outs),
        compiler_params=pltpu.CompilerParams(vmem_limit_bytes=mib * MIB),
        **more,
    )(*args)


def on_device(latents, queries, hot_ids, lengths):
    by_column = latents.T
    count = queries.shape[0]
    chunk, pair = ((WIDTH, CHUNK), bf16), ((WIDTH, PAIR), bf16)

    up, down = call(
        first_cut_kernel,
        [pair, pair],
        [SMEM, ANY],
        [hot_ids, by_column],
        mib=50,
        scratch_shapes=[pltpu.SemaphoreType.DMA((4,))],
    )
    up, down = shift_rep(up, 1), shift_rep(down, -1)
    own = queries.reshape(count, -1, WIDTH).transpose(1, 0, 2).reshape(-1, WIDTH)
    near = jnp.concatenate([own, cross_z(own, 2)], axis=0)
    right, left, mine = call(
        own_cut_kernel,
        [chunk] * 3,
        [SMEM, ANY],
        [hot_ids, by_column],
        mib=50,
        scratch_shapes=[pltpu.SemaphoreType.DMA((12,))],
    )
    up, down, near = lax.optimization_barrier((up, down, near))
    right, left = call(
        pass_on_kernel,
        [chunk] * 2,
        [SMEM] + [VMEM] * 4,
        [hot_ids, up, down, right, left],
    )
    from_left, from_right = shift_rep(right, 1), shift_rep(left, -1)
    for bits in (4, 1):
        near = jnp.concatenate([near, cross_z(near, bits)], axis=0)
    from_left, from_right, near = lax.optimization_barrier((from_left, from_right, near))
    (mine,) = call(
        settle_kernel,
        [chunk],
        [SMEM] + [VMEM] * 3,
        [hot_ids, from_left, from_right, mine],
    )
    asked = [near] + [cross_x(near, bits) for bits in range(1, N_X)]
    hot_other = swap_core(hot_ids)

    of_left, of_right = shift_rep(mine, 1), shift_rep(mine, -1)
    of_left, of_right, *asked = lax.optimization_barrier((of_left, of_right, *asked))
    far_a, far_b = shift_rep(of_left[:, :PAIR], 1), shift_rep(of_right[:, PAIR:], -1)
    keys = [mine, of_left, of_right]
    swapped = [swap_core(k) for k in keys]

    rows = near.shape[0]
    scores = []
    for other, (hot, some) in enumerate(((hot_ids, keys), (hot_other, swapped))):
        found = call(
            functools.partial(score_kernel, other),
            [((rows, len(NEAR) * CHUNK), f32), ((rows, 128), f32)] * N_X,
            [SMEM, SMEM] + [VMEM] * (N_X + len(NEAR)),
            [lengths, hot, *asked, *some],
            flops=2 * N_X * rows * WIDTH * len(NEAR) * CHUNK,
        )
        scores.append([found[2 * hop : 2 * hop + 2] for hop in range(N_X)])
    scores, far_a, far_b = lax.optimization_barrier((scores, far_a, far_b))
    keys += [far_a, far_b]
    swapped += [swap_core(far_a), swap_core(far_b)]

    rows = rows // 2
    part = ((rows + STAT_ROWS, LAT), bf16)
    parts = []
    for i, hop in enumerate((2, 1, 3, 0)):
        if i > 1:
            lengths, *sent = lax.optimization_barrier((lengths, *parts[2 * i - 4 : 2 * i - 2]))
            parts[2 * i - 4 : 2 * i - 2] = sent
        same, flipped = call(
            attend_kernel,
            [part, part],
            [VMEM] * 5 + [SMEM] * 3 + [VMEM] * (N_C * len(keys)),
            [asked[hop], *scores[0][hop], *scores[1][hop], lengths, hot_ids, hot_other, *keys, *swapped],
            flops=4 * rows * (LAT + WIDTH // 4) * N_C * N_REP * CHUNK,
        )
        lengths, same, flipped = lax.optimization_barrier((lengths, same, flipped))
        parts.append(cross_xz(flipped, hop, 1))
        parts.append(cross_xz(same, hop, 0) if hop else same)

    n = own.shape[0]
    message = ((n, LAT + 128), bf16)
    *sends, mine, stat = call(
        merge_kernel,
        [message] * (N_FAR - 1) + [((n, LAT), f32), ((n, 128), f32)],
        [VMEM] * len(parts),
        parts,
    )
    sends = [cross_z(s, 2 * far) for far, s in enumerate(sends, 1)]
    (out,) = call(
        finish_kernel,
        [((count, n // count * LAT), bf16)],
        [VMEM] * (2 + len(sends)),
        [mine, stat, *sends],
    )
    return out


def solution(mesh):
    assert dict(mesh.shape) == {"ctx": N_X * N_Z * N_C, "rep": N_REP}
    split = Mesh(mesh.devices.reshape(N_X, N_Z, N_C, N_REP), ("x", "z", "c", "rep"))
    ctx = ("x", "z", "c")
    placed = (P((*ctx, "rep"), None), P("rep", ctx), P(ctx), P("rep"))
    return jax.shard_map(
        on_device, mesh=split, in_specs=placed, out_specs=P("rep", ctx), check_vma=False
    )
```

```python
import functools

import jax
import jax.numpy as jnp
from jax import lax
from jax.experimental import pallas as pl
from jax.experimental.pallas import tpu as pltpu
from jax.sharding import Mesh, PartitionSpec as P

H = 128
LAT = 512
ROPE = 64
QK = 192
BLK = 1024
HOT_GRP = 2
BPG = 16
WIDTH = LAT + ROPE
N_X = 4
N_Z = 8
N_C = 2
N_REP = 4
PER_DEV = BPG // N_REP
QUARTER = BLK // N_REP
HALF = QUARTER // 2
PAIR = HOT_GRP * HALF
CHUNK = 2 * PAIR
NEVER = -1e30
STAT_ROWS = 8
Z_ORDER = (0, 4, 2, 6)
SCALE = QK**-0.5
LOG2_E = 1.4426950408889634
N_FAR = N_Z // 2
f32 = jnp.float32
bf16 = jnp.bfloat16

VMEM = pl.BlockSpec(memory_space=pltpu.VMEM)
SMEM = pl.BlockSpec(memory_space=pltpu.SMEM)
ANY = pl.BlockSpec(memory_space=pltpu.HBM)
MIB = 1024 * 1024


def shift_rep(a, by):
    return lax.ppermute(a, "rep", [(i, (i + by) % N_REP) for i in range(N_REP)])


def swap_core(a):
    return lax.ppermute(a, "c", [(0, 1), (1, 0)])


def cross_x(a, bits):
    return lax.ppermute(a, "x", [(i, i ^ bits) for i in range(N_X)])


def cross_z(a, bits):
    return lax.ppermute(a, ("zf", "zp"), [(i, i ^ bits) for i in range(N_Z)])


def cross_xz(a, bits_x, bits_z):
    pairs = []
    for x in range(N_X):
        for z in range(N_Z):
            pairs.append((x * N_Z + z, (x ^ bits_x) * N_Z + (z ^ bits_z)))
    return lax.ppermute(a, ("x", "zf", "zp"), pairs)


def column(hot_ref, slot, rank, half):
    at = hot_ref[slot] % PER_DEV * BLK + rank * QUARTER + half * HALF
    return pl.ds(pl.multiple_of(at, HALF), HALF)


def run_copies(copies):
    for c in copies:
        c.start()
    for c in copies:
        c.wait()


def first_cut_kernel(hot_ref, lat_ref, up_ref, down_ref, sems):
    far = (lax.axis_index("rep") + 2) % N_REP
    copies = []
    for half, dst in enumerate((up_ref, down_ref)):
        for slot in range(HOT_GRP):
            copies.append(
                pltpu.make_async_copy(
                    lat_ref.at[:, column(hot_ref, slot, far, half)],
                    dst.at[:, pl.ds(slot * HALF, HALF)],
                    sems.at[len(copies)],
                )
            )
    run_copies(copies)


def own_cut_kernel(hot_ref, lat_ref, right_ref, left_ref, mine_ref, sems):
    rank = lax.axis_index("rep")
    copies = []
    for hop, dst in ((1, right_ref), (3, left_ref), (0, mine_ref)):
        for half in range(2):
            for slot in range(HOT_GRP):
                copies.append(
                    pltpu.make_async_copy(
                        lat_ref.at[:, column(hot_ref, slot, (rank + hop) % N_REP, half)],
                        dst.at[:, pl.ds(half * PAIR + slot * HALF, HALF)],
                        sems.at[len(copies)],
                    )
                )
    run_copies(copies)


def pass_on_kernel(hot_ref, from_left, from_right, right_in, left_in, right_ref, left_ref):
    rank = lax.axis_index("rep")
    right_ref[:, PAIR:] = right_in[:, PAIR:]
    left_ref[:, :PAIR] = left_in[:, :PAIR]
    for slot in range(HOT_GRP):
        a = slice(slot * HALF, (slot + 1) * HALF)
        b = slice(PAIR + slot * HALF, PAIR + (slot + 1) * HALF)
        here = hot_ref[slot] // PER_DEV == rank

        @pl.when(here)
        def _():
            right_ref[:, a] = right_in[:, a]
            left_ref[:, b] = left_in[:, b]

        @pl.when(jnp.logical_not(here))
        def _():
            right_ref[:, a] = from_left[:, a]
            left_ref[:, b] = from_right[:, a]


def settle_kernel(hot_ref, from_left, from_right, mine_in, mine_ref):
    rank = lax.axis_index("rep")
    for slot in range(HOT_GRP):
        a = slice(slot * HALF, (slot + 1) * HALF)
        b = slice(PAIR + slot * HALF, PAIR + (slot + 1) * HALF)
        away = (hot_ref[slot] // PER_DEV - rank + N_REP) % N_REP

        @pl.when(away == 0)
        def _():
            mine_ref[:, a] = mine_in[:, a]
            mine_ref[:, b] = mine_in[:, b]

        @pl.when(away >= 2)
        def _():
            mine_ref[:, a] = from_left[:, a]

        @pl.when(away == 1)
        def _():
            mine_ref[:, a] = from_right[:, a]

        @pl.when(away == 3)
        def _():
            mine_ref[:, b] = from_left[:, b]

        @pl.when((away == 1) | (away == 2))
        def _():
            mine_ref[:, b] = from_right[:, b]


def three_terms(v):
    hi = v.astype(bf16)
    mid = (v - hi.astype(f32)).astype(bf16)
    low = (v - hi.astype(f32) - mid.astype(f32)).astype(bf16)
    return [hi, mid, low]


def visible_lengths(len_ref, rows):
    count = len_ref.shape[0]
    line = lax.broadcasted_iota(jnp.int32, (count, 1), 0)
    lens = jnp.zeros((count, 1), jnp.int32)
    for i in range(count):
        lens = jnp.where(line == i, len_ref[i], lens)
    return jnp.concatenate([lens] * (rows // count), axis=0)


def row_numbers(hot_ref, other, away, half, halves):
    x, c = lax.axis_index("x"), lax.axis_index("c")
    z = lax.axis_index("zf") * 2 + lax.axis_index("zp")
    group = (x * N_Z + z) * N_C + c + other * (1 - 2 * c)
    at = (lax.axis_index("rep") + away) % N_REP * QUARTER
    lane = lax.broadcasted_iota(jnp.int32, (1, HALF), 1)
    return jnp.concatenate(
        [
            (group * BPG + hot_ref[slot]) * BLK + at + h * HALF + lane
            for h in range(half, half + halves)
            for slot in range(HOT_GRP)
        ],
        axis=1,
    )


NEAR = (0, 3, 1)
FAR = 2


def fold(op, s):
    return functools.reduce(op, [s[:, i : i + 128] for i in range(0, s.shape[1], 128)])


def score_kernel(other, len_ref, hot_ref, *refs):
    q_refs, key_refs, outs = refs[:N_X], refs[N_X : N_X + len(NEAR)], refs[N_X + len(NEAR) :]
    lens = visible_lengths(len_ref, q_refs[0].shape[0])
    rows = [row_numbers(hot_ref, other, away, 0, 2) for away in NEAR]
    for i, q_ref in enumerate(q_refs):
        s_ref, peak_ref = outs[2 * i : 2 * i + 2]
        q = q_ref[...]
        peaks = []
        for j, k_ref in enumerate(key_refs):
            s = jnp.dot(q, k_ref[...], preferred_element_type=f32)
            s = jnp.where(rows[j] < lens, s, NEVER)
            s_ref[:, j * CHUNK : (j + 1) * CHUNK] = s
            peaks.append(fold(jnp.maximum, s))
        peak_ref[...] = functools.reduce(jnp.maximum, peaks)


def attend_kernel(halves, *refs):
    n = len(NEAR)
    q_refs, s_refs, refs = refs[:2], refs[2:10], refs[10:]
    (len_ref, *hot_refs), refs = refs[:3], refs[3:]
    key_refs, outs = refs[: N_C * (n + 2)], refs[N_C * (n + 2) :]
    span = q_refs[0].shape[0] // 2
    cuts = [slice(half * span, (half + 1) * span) for half in halves]

    def two(a_ref, b_ref, columns=slice(None)):
        return jnp.concatenate([a_ref[cuts[0], columns], b_ref[cuts[1], columns]], axis=0)

    q = two(*q_refs)
    lens = visible_lengths(len_ref, q.shape[0])
    last = []
    for other in range(N_C):
        for half in range(2):
            k_ref = key_refs[other * (n + 2) + n + half]
            rows = row_numbers(hot_refs[other], other, FAR, half, 1)
            s = jnp.dot(q, k_ref[...], preferred_element_type=f32)
            last.append(jnp.where(rows < lens, s, NEVER))
    parts = []
    for other in range(N_C):
        keys = key_refs[other * (n + 2) : (other + 1) * (n + 2)]
        s_pair = s_refs[other * 4 : other * 4 + 4 : 2]
        scores = [two(*s_pair, slice(i * CHUNK, (i + 1) * CHUNK)) for i in range(n)]
        scores += last[other * 2 : other * 2 + 2]
        peak = two(*s_refs[other * 4 + 1 : other * 4 + 4 : 2])
        for s in last[other * 2 : other * 2 + 2]:
            peak = jnp.maximum(peak, fold(jnp.maximum, s))
        peak = peak.max(axis=1, keepdims=True)
        total = 0.0
        numer = None
        for s, k_ref in zip(scores, keys):
            w = jnp.exp2((s - peak) * (SCALE * LOG2_E)).astype(bf16)
            total = total + fold(jnp.add, w.astype(f32))
            v = lax.dot_general(
                w, k_ref[:LAT, :], (((1,), (1,)), ((), ())), preferred_element_type=f32
            )
            numer = v if numer is None else numer + v
        parts.append((peak, total.sum(axis=1, keepdims=True), numer))
    top = jnp.maximum(parts[0][0], parts[1][0])
    numer, total = 0.0, 0.0
    for peak, t, v in parts:
        f = jnp.where(peak > NEVER / 2, jnp.exp((peak - top) * SCALE), 0.0)
        numer = numer + v * f
        total = total + t * f
    o = (numer * (1.0 / jnp.maximum(total, 1.0))).astype(bf16)
    lanes = lax.broadcasted_iota(jnp.int32, (q.shape[0], 128), 1)
    stats = jnp.where(lanes == 0, top * SCALE, total).T[:2, :]
    for flip, o_ref in enumerate(outs):
        o_ref[:span, :] = o[flip * span : (flip + 1) * span]
        mine = stats[:, flip * span : (flip + 1) * span]
        terms = three_terms(mine[0:1]) + three_terms(mine[1:2])
        terms = [t.astype(f32) for t in terms] + [jnp.zeros((STAT_ROWS - 6, span), f32)]
        o_ref[span:, :span] = jnp.concatenate(terms, axis=0).astype(bf16)
        o_ref[span:, span:] = jnp.zeros((STAT_ROWS, LAT - span), bf16)


def merge_kernel(*refs):
    parts, out_ref = refs[:-1], refs[-1]
    n_in = len(parts)
    rows = parts[0].shape[0] - STAT_ROWS
    tops, totals = [], []
    for p in parts:
        s = p[rows:, :rows].astype(f32)
        tops.append(s[0:1] + s[1:2] + s[2:3])
        totals.append(s[3:4] + s[4:5] + s[5:6])
    top = functools.reduce(jnp.maximum, tops)
    weights = [t * jnp.exp(m - top) for m, t in zip(tops, totals)]
    total = sum(weights)
    inv = 1.0 / jnp.maximum(total, 1.0)
    table = [w * inv for w in weights] + [top, total]
    table.append(jnp.zeros((128 - len(table), rows), f32))
    table = jnp.concatenate(table, axis=0).T
    n = rows // N_FAR
    lane = lax.broadcasted_iota(jnp.int32, (n, 128), 1)
    for i, bits in enumerate(Z_ORDER):
        at = slice(i * n, (i + 1) * n)
        acc = 0.0
        for j, p in enumerate(parts):
            acc = acc + p[at, :].astype(f32) * table[at, j : j + 1]
        to = pl.ds(pl.multiple_of((lax.axis_index("zf") ^ (bits // 2)) * n, n), n)
        out_ref[to, :LAT] = acc.astype(bf16)
        packed = jnp.zeros((n, 128), f32)
        terms = three_terms(table[at, n_in : n_in + 1])
        terms += three_terms(table[at, n_in + 1 : n_in + 2])
        for j, term in enumerate(terms):
            packed = jnp.where(lane == j, term.astype(f32), packed)
        out_ref[to, LAT:] = packed.astype(bf16)


def finish_kernel(in_ref, out_ref):
    n = in_ref.shape[0] // N_FAR
    parts = [in_ref[i * n : (i + 1) * n, :].astype(f32) for i in range(N_FAR)]
    tops, totals = [], []
    for p in parts:
        s = p[:, LAT:]
        tops.append(s[:, 0:1] + s[:, 1:2] + s[:, 2:3])
        totals.append(s[:, 3:4] + s[:, 4:5] + s[:, 5:6])
    top = functools.reduce(jnp.maximum, tops)
    weights = [t * jnp.exp(m - top) for m, t in zip(tops, totals)]
    o = sum(p[:, :LAT] * w for p, w in zip(parts, weights)) / sum(weights)
    count = out_ref.shape[0]
    for head in range(n // count):
        out_ref[:, head * LAT : (head + 1) * LAT] = o[head * count : (head + 1) * count].astype(bf16)


def call(kernel, outs, in_specs, args, mib=16, flops=0, **more):
    if flops:
        more["cost_estimate"] = pl.CostEstimate(
            flops=flops, bytes_accessed=8 * MIB, transcendentals=0
        )
    return pl.pallas_call(
        kernel,
        out_shape=tuple(jax.ShapeDtypeStruct(*o) for o in outs),
        in_specs=in_specs,
        out_specs=(VMEM,) * len(outs),
        compiler_params=pltpu.CompilerParams(vmem_limit_bytes=mib * MIB),
        **more,
    )(*args)


def on_device(latents, queries, hot_ids, lengths):
    by_column = latents.T
    count = queries.shape[0]
    chunk, pair = ((WIDTH, CHUNK), bf16), ((WIDTH, PAIR), bf16)

    up, down = call(
        first_cut_kernel,
        [pair, pair],
        [SMEM, ANY],
        [hot_ids, by_column],
        mib=50,
        scratch_shapes=[pltpu.SemaphoreType.DMA((4,))],
    )
    up, down = shift_rep(up, 1), shift_rep(down, -1)
    own = queries.reshape(count, -1, WIDTH).transpose(1, 0, 2).reshape(-1, WIDTH)
    near = jnp.concatenate([own, cross_z(own, 4)], axis=0)
    right, left, mine = call(
        own_cut_kernel,
        [chunk] * 3,
        [SMEM, ANY],
        [hot_ids, by_column],
        mib=50,
        scratch_shapes=[pltpu.SemaphoreType.DMA((12,))],
    )
    up, down, near = lax.optimization_barrier((up, down, near))
    right, left = call(
        pass_on_kernel,
        [chunk] * 2,
        [SMEM] + [VMEM] * 4,
        [hot_ids, up, down, right, left],
    )
    from_left, from_right = shift_rep(right, 1), shift_rep(left, -1)
    for bits in (2, 1):
        near = jnp.concatenate([near, cross_z(near, bits)], axis=0)
    (mine,) = call(
        settle_kernel,
        [chunk],
        [SMEM] + [VMEM] * 3,
        [hot_ids, from_left, from_right, mine],
    )
    asked = [near] + [cross_x(near, bits) for bits in range(1, N_X)]
    hot_other = swap_core(hot_ids)

    of_left, of_right = shift_rep(mine, 1), shift_rep(mine, -1)
    of_left, of_right, *asked = lax.optimization_barrier((of_left, of_right, *asked))
    far_a, far_b = shift_rep(of_left[:, :PAIR], 1), shift_rep(of_right[:, PAIR:], -1)
    keys = [mine, of_left, of_right]
    swapped = [swap_core(k) for k in keys]

    rows = near.shape[0]
    scores = []
    for other, (hot, some) in enumerate(((hot_ids, keys), (hot_other, swapped))):
        found = call(
            functools.partial(score_kernel, other),
            [((rows, len(NEAR) * CHUNK), f32), ((rows, 128), f32)] * N_X,
            [SMEM, SMEM] + [VMEM] * (N_X + len(NEAR)),
            [lengths, hot, *asked, *some],
            flops=2 * N_X * rows * WIDTH * len(NEAR) * CHUNK,
        )
        scores.append([found[2 * hop : 2 * hop + 2] for hop in range(N_X)])
    scores, far_a, far_b = lax.optimization_barrier((scores, far_a, far_b))
    keys += [far_a, far_b]
    swapped += [swap_core(far_a), swap_core(far_b)]

    rows = rows // 2
    part = ((rows + STAT_ROWS, LAT), bf16)
    parts = []
    for i, pair_of in enumerate((((2, 0), (2, 1)), ((1, 0), (3, 0)), ((1, 1), (3, 1)), ((0, 1), (0, 0)))):
        if i > 1:
            lengths, *sent = lax.optimization_barrier((lengths, *parts[2 * i - 4 : 2 * i - 2]))
            parts[2 * i - 4 : 2 * i - 2] = sent
        (hop_a, half_a), (hop_b, half_b) = pair_of
        found = [a for group in scores for hop in (hop_a, hop_b) for a in group[hop]]
        first, second = call(
            functools.partial(attend_kernel, (half_a, half_b)),
            [part, part],
            [VMEM] * 10 + [SMEM] * 3 + [VMEM] * (N_C * len(keys)),
            [asked[hop_a], asked[hop_b], *found, lengths, hot_ids, hot_other, *keys, *swapped],
            flops=4 * rows * (LAT + WIDTH // 4) * N_C * N_REP * CHUNK,
        )
        lengths, first, second = lax.optimization_barrier((lengths, first, second))
        if hop_b == 0:
            first, *sent = lax.optimization_barrier((first, *parts[2 * i - 2 :]))
            parts[2 * i - 2 :] = sent
        for value, (hop, half) in zip((first, second), pair_of):
            parts.append(cross_xz(value, hop, half) if hop or half else value)

    message = ((rows, LAT + 128), bf16)
    (merged,) = call(merge_kernel, [message], [VMEM] * len(parts), parts)
    merged = lax.all_to_all(merged, "zf", 0, 0, tiled=True)
    (out,) = call(
        finish_kernel, [((count, own.shape[0] // count * LAT), bf16)], [VMEM], [merged]
    )
    return out


def solution(mesh):
    assert dict(mesh.shape) == {"ctx": N_X * N_Z * N_C, "rep": N_REP}
    split = Mesh(
        mesh.devices.reshape(N_X, N_FAR, 2, N_C, N_REP), ("x", "zf", "zp", "c", "rep")
    )
    ctx = ("x", "zf", "zp", "c")
    placed = (P((*ctx, "rep"), None), P("rep", ctx), P(ctx), P("rep"))
    return jax.shard_map(
        on_device, mesh=split, in_specs=placed, out_specs=P("rep", ctx), check_vma=False
    )
```

```python
import functools

import jax
import jax.numpy as jnp
from jax import lax
from jax.experimental import pallas as pl
from jax.experimental.pallas import tpu as pltpu
from jax.sharding import Mesh, PartitionSpec as P

H = 128
LAT = 512
ROPE = 64
QK = 192
BLK = 1024
HOT_GRP = 2
BPG = 16
WIDTH = LAT + ROPE
N_X = 4
N_Z = 8
N_C = 2
N_REP = 4
PER_DEV = BPG // N_REP
QUARTER = BLK // N_REP
HALF = QUARTER // 2
PAIR = HOT_GRP * HALF
CHUNK = 2 * PAIR
NEVER = -1e30
STAT_ROWS = 8
Z_ORDER = (0, 4, 2, 6, 1, 5, 3, 7)
SCALE = QK**-0.5
LOG2_E = 1.4426950408889634
N_FAR = N_Z // 2
f32 = jnp.float32
bf16 = jnp.bfloat16

VMEM = pl.BlockSpec(memory_space=pltpu.VMEM)
SMEM = pl.BlockSpec(memory_space=pltpu.SMEM)
ANY = pl.BlockSpec(memory_space=pltpu.HBM)
MIB = 1024 * 1024


def shift_rep(a, by):
    return lax.ppermute(a, "rep", [(i, (i + by) % N_REP) for i in range(N_REP)])


def swap_core(a):
    return lax.ppermute(a, "c", [(0, 1), (1, 0)])


def cross_x(a, bits):
    return lax.ppermute(a, "x", [(i, i ^ bits) for i in range(N_X)])


def cross_z(a, bits):
    return lax.ppermute(a, "z", [(i, i ^ bits) for i in range(N_Z)])


def column(hot_ref, slot, rank, half):
    at = hot_ref[slot] % PER_DEV * BLK + rank * QUARTER + half * HALF
    return pl.ds(pl.multiple_of(at, HALF), HALF)


def run_copies(copies):
    for c in copies:
        c.start()
    for c in copies:
        c.wait()


def first_cut_kernel(hot_ref, lat_ref, up_ref, down_ref, sems):
    far = (lax.axis_index("rep") + 2) % N_REP
    copies = []
    for half, dst in enumerate((up_ref, down_ref)):
        for slot in range(HOT_GRP):
            copies.append(
                pltpu.make_async_copy(
                    lat_ref.at[:, column(hot_ref, slot, far, half)],
                    dst.at[:, pl.ds(slot * HALF, HALF)],
                    sems.at[len(copies)],
                )
            )
    run_copies(copies)


def own_cut_kernel(hot_ref, lat_ref, right_ref, left_ref, mine_ref, sems):
    rank = lax.axis_index("rep")
    copies = []
    for hop, dst in ((1, right_ref), (3, left_ref), (0, mine_ref)):
        for half in range(2):
            for slot in range(HOT_GRP):
                copies.append(
                    pltpu.make_async_copy(
                        lat_ref.at[:, column(hot_ref, slot, (rank + hop) % N_REP, half)],
                        dst.at[:, pl.ds(half * PAIR + slot * HALF, HALF)],
                        sems.at[len(copies)],
                    )
                )
    run_copies(copies)


def pass_on_kernel(hot_ref, from_left, from_right, right_in, left_in, right_ref, left_ref):
    rank = lax.axis_index("rep")
    right_ref[:, PAIR:] = right_in[:, PAIR:]
    left_ref[:, :PAIR] = left_in[:, :PAIR]
    for slot in range(HOT_GRP):
        a = slice(slot * HALF, (slot + 1) * HALF)
        b = slice(PAIR + slot * HALF, PAIR + (slot + 1) * HALF)
        here = hot_ref[slot] // PER_DEV == rank

        @pl.when(here)
        def _():
            right_ref[:, a] = right_in[:, a]
            left_ref[:, b] = left_in[:, b]

        @pl.when(jnp.logical_not(here))
        def _():
            right_ref[:, a] = from_left[:, a]
            left_ref[:, b] = from_right[:, a]


def settle_kernel(hot_ref, from_left, from_right, mine_in, mine_ref):
    rank = lax.axis_index("rep")
    for slot in range(HOT_GRP):
        a = slice(slot * HALF, (slot + 1) * HALF)
        b = slice(PAIR + slot * HALF, PAIR + (slot + 1) * HALF)
        away = (hot_ref[slot] // PER_DEV - rank + N_REP) % N_REP

        @pl.when(away == 0)
        def _():
            mine_ref[:, a] = mine_in[:, a]
            mine_ref[:, b] = mine_in[:, b]

        @pl.when(away >= 2)
        def _():
            mine_ref[:, a] = from_left[:, a]

        @pl.when(away == 1)
        def _():
            mine_ref[:, a] = from_right[:, a]

        @pl.when(away == 3)
        def _():
            mine_ref[:, b] = from_left[:, b]

        @pl.when((away == 1) | (away == 2))
        def _():
            mine_ref[:, b] = from_right[:, b]


def three_terms(v):
    hi = v.astype(bf16)
    mid = (v - hi.astype(f32)).astype(bf16)
    low = (v - hi.astype(f32) - mid.astype(f32)).astype(bf16)
    return [hi, mid, low]


def visible_lengths(len_ref, rows):
    count = len_ref.shape[0]
    line = lax.broadcasted_iota(jnp.int32, (count, 1), 0)
    lens = jnp.zeros((count, 1), jnp.int32)
    for i in range(count):
        lens = jnp.where(line == i, len_ref[i], lens)
    return jnp.concatenate([lens] * (rows // count), axis=0)


def row_numbers(hot_ref, other, away, half, halves):
    x, z, c = lax.axis_index("x"), lax.axis_index("z"), lax.axis_index("c")
    group = (x * N_Z + z) * N_C + c + other * (1 - 2 * c)
    at = (lax.axis_index("rep") + away) % N_REP * QUARTER
    lane = lax.broadcasted_iota(jnp.int32, (1, HALF), 1)
    return jnp.concatenate(
        [
            (group * BPG + hot_ref[slot]) * BLK + at + h * HALF + lane
            for h in range(half, half + halves)
            for slot in range(HOT_GRP)
        ],
        axis=1,
    )


PLACES = ((0, 0, 2), (3, 0, 2), (1, 0, 2), (2, 0, 1), (2, 1, 1))


def fold(op, s):
    return functools.reduce(op, [s[:, i : i + 128] for i in range(0, s.shape[1], 128)])


def attend_kernel(q_ref, len_ref, hot_ref, hot_other_ref, *refs):
    n = len(PLACES)
    key_refs, o_ref = refs[:-1], refs[-1]
    q = q_ref[...]
    lens = visible_lengths(len_ref, q.shape[0])
    parts = []
    for other, hot in enumerate((hot_ref, hot_other_ref)):
        keys = key_refs[other * n : (other + 1) * n]
        scores = []
        for k_ref, place in zip(keys, PLACES):
            numbers = row_numbers(hot, other, *place)
            s = jnp.dot(q, k_ref[...], preferred_element_type=f32)
            scores.append(jnp.where(numbers < lens, s, NEVER))
        peak = functools.reduce(jnp.maximum, [fold(jnp.maximum, s) for s in scores])
        peak = peak.max(axis=1, keepdims=True)
        total = 0.0
        numer = None
        for s, k_ref in zip(scores, keys):
            w = jnp.exp2((s - peak) * (SCALE * LOG2_E)).astype(bf16)
            total = total + fold(jnp.add, w.astype(f32))
            v = lax.dot_general(
                w, k_ref[:LAT, :], (((1,), (1,)), ((), ())), preferred_element_type=f32
            )
            numer = v if numer is None else numer + v
        parts.append((peak, total.sum(axis=1, keepdims=True), numer))
    top = jnp.maximum(parts[0][0], parts[1][0])
    numer, total = 0.0, 0.0
    for peak, t, v in parts:
        f = jnp.where(peak > NEVER / 2, jnp.exp((peak - top) * SCALE), 0.0)
        numer = numer + v * f
        total = total + t * f
    o = (numer * (1.0 / jnp.maximum(total, 1.0))).astype(bf16)
    rows = q.shape[0]
    lanes = lax.broadcasted_iota(jnp.int32, (rows, 128), 1)
    stats = jnp.where(lanes == 0, top * SCALE, total).T[:2, :]
    terms = three_terms(stats[0:1]) + three_terms(stats[1:2])
    terms = [t.astype(f32) for t in terms] + [jnp.zeros((STAT_ROWS - 6, rows), f32)]
    o_ref[:rows, :] = o
    o_ref[rows:, :rows] = jnp.concatenate(terms, axis=0).astype(bf16)
    o_ref[rows:, rows:] = jnp.zeros((STAT_ROWS, LAT - rows), bf16)


def merge_kernel(*refs):
    parts, outs = refs[:N_X], refs[N_X:]
    rows = parts[0].shape[0] - STAT_ROWS
    tops, totals = [], []
    for p in parts:
        s = p[rows:, :rows].astype(f32)
        tops.append(s[0:1] + s[1:2] + s[2:3])
        totals.append(s[3:4] + s[4:5] + s[5:6])
    top = functools.reduce(jnp.maximum, tops)
    weights = [t * jnp.exp(m - top) for m, t in zip(tops, totals)]
    total = sum(weights)
    inv = 1.0 / jnp.maximum(total, 1.0)
    table = [w * inv for w in weights] + [top, total]
    table.append(jnp.zeros((128 - len(table), rows), f32))
    table = jnp.concatenate(table, axis=0).T
    n = rows // N_Z
    lane = lax.broadcasted_iota(jnp.int32, (n, 128), 1)
    for i, ref in enumerate(outs):
        at = slice(i * n, (i + 1) * n)
        acc = 0.0
        for j, p in enumerate(parts):
            acc = acc + p[at, :].astype(f32) * table[at, j : j + 1]
        ref[:, :LAT] = acc.astype(ref.dtype)
        packed = jnp.zeros((n, 128), f32)
        terms = three_terms(table[at, N_X : N_X + 1])
        terms += three_terms(table[at, N_X + 1 : N_X + 2])
        for j, term in enumerate(terms):
            packed = jnp.where(lane == j, term.astype(f32), packed)
        ref[:, LAT:] = packed.astype(ref.dtype)


def finish_kernel(*refs):
    parts, out_ref = [r[...].astype(f32) for r in refs[:-1]], refs[-1]
    tops, totals = [], []
    for p in parts:
        s = p[:, LAT:]
        tops.append(s[:, 0:1] + s[:, 1:2] + s[:, 2:3])
        totals.append(s[:, 3:4] + s[:, 4:5] + s[:, 5:6])
    top = functools.reduce(jnp.maximum, tops)
    weights = [t * jnp.exp(m - top) for m, t in zip(tops, totals)]
    o = sum(p[:, :LAT] * w for p, w in zip(parts, weights)) / sum(weights)
    count = out_ref.shape[0]
    for head in range(o.shape[0] // count):
        out_ref[:, head * LAT : (head + 1) * LAT] = o[head * count : (head + 1) * count].astype(bf16)


def call(kernel, outs, in_specs, args, mib=16, **more):
    return pl.pallas_call(
        kernel,
        out_shape=tuple(jax.ShapeDtypeStruct(*o) for o in outs),
        in_specs=in_specs,
        out_specs=(VMEM,) * len(outs),
        compiler_params=pltpu.CompilerParams(vmem_limit_bytes=mib * MIB),
        **more,
    )(*args)


def on_device(latents, queries, hot_ids, lengths):
    by_column = latents.T
    count = queries.shape[0]
    chunk, pair = ((WIDTH, CHUNK), bf16), ((WIDTH, PAIR), bf16)

    up, down = call(
        first_cut_kernel,
        [pair, pair],
        [SMEM, ANY],
        [hot_ids, by_column],
        mib=50,
        scratch_shapes=[pltpu.SemaphoreType.DMA((4,))],
    )
    up, down = shift_rep(up, 1), shift_rep(down, -1)
    own = queries.reshape(count, -1, WIDTH).transpose(1, 0, 2).reshape(-1, WIDTH)
    near = jnp.concatenate([own, cross_z(own, 4)], axis=0)
    right, left, mine = call(
        own_cut_kernel,
        [chunk] * 3,
        [SMEM, ANY],
        [hot_ids, by_column],
        mib=50,
        scratch_shapes=[pltpu.SemaphoreType.DMA((12,))],
    )
    up, down, near = lax.optimization_barrier((up, down, near))
    right, left = call(
        pass_on_kernel,
        [chunk] * 2,
        [SMEM] + [VMEM] * 4,
        [hot_ids, up, down, right, left],
    )
    from_left, from_right = shift_rep(right, 1), shift_rep(left, -1)
    for bits in (2, 1):
        near = jnp.concatenate([near, cross_z(near, bits)], axis=0)
    (mine,) = call(
        settle_kernel,
        [chunk],
        [SMEM] + [VMEM] * 3,
        [hot_ids, from_left, from_right, mine],
    )
    asked = [near] + [cross_x(near, bits) for bits in range(1, N_X)]
    hot_other = swap_core(hot_ids)

    of_left, of_right = shift_rep(mine, 1), shift_rep(mine, -1)
    far_a, far_b = shift_rep(of_left[:, :PAIR], 1), shift_rep(of_right[:, PAIR:], -1)
    far_a, far_b, *asked = lax.optimization_barrier((far_a, far_b, *asked))
    keys = [mine, of_left, of_right, far_a, far_b]
    keys = keys + [swap_core(k) for k in keys]

    rows = near.shape[0]
    parts = []
    for i, hop in enumerate((2, 1, 3, 0)):
        if i > 1:
            lengths, parts[i - 2] = lax.optimization_barrier((lengths, parts[i - 2]))
        (o,) = call(
            attend_kernel,
            [((rows + STAT_ROWS, LAT), bf16)],
            [VMEM, SMEM, SMEM, SMEM] + [VMEM] * len(keys),
            [asked[hop], lengths, hot_ids, hot_other, *keys],
        )
        lengths, o = lax.optimization_barrier((lengths, o))
        parts.append(cross_x(o, hop) if hop else o)

    n = own.shape[0]
    ours, *sends = call(
        merge_kernel,
        [((n, LAT + 128), f32 if i == 0 else bf16) for i in range(N_Z)],
        [VMEM] * N_X,
        parts,
    )
    sends = [cross_z(s, bits) for s, bits in zip(sends, Z_ORDER[1:])]
    (out,) = call(
        finish_kernel,
        [((count, n // count * LAT), bf16)],
        [VMEM] * N_Z,
        [ours, *sends],
    )
    return out


def solution(mesh):
    assert dict(mesh.shape) == {"ctx": N_X * N_Z * N_C, "rep": N_REP}
    split = Mesh(mesh.devices.reshape(N_X, N_Z, N_C, N_REP), ("x", "z", "c", "rep"))
    ctx = ("x", "z", "c")
    placed = (P((*ctx, "rep"), None), P("rep", ctx), P(ctx), P("rep"))
    return jax.shard_map(
        on_device, mesh=split, in_specs=placed, out_specs=P("rep", ctx), check_vma=False
    )
```

```python
import functools

import jax
import jax.numpy as jnp
from jax import lax
from jax.experimental import pallas as pl
from jax.experimental.pallas import tpu as pltpu
from jax.sharding import Mesh, PartitionSpec as P

H = 128
LAT = 512
ROPE = 64
QK = 192
BLK = 1024
HOT_GRP = 2
BPG = 16
WIDTH = LAT + ROPE
N_X = 4
N_Z = 8
N_C = 2
N_REP = 4
PER_DEV = BPG // N_REP
QUARTER = BLK // N_REP
HALF = QUARTER // 2
PAIR = HOT_GRP * HALF
CHUNK = 2 * PAIR
NEVER = -1e30
STAT_ROWS = 8
Z_ORDER = (0, 4, 2, 6, 1, 5, 3, 7)
SCALE = QK**-0.5
LOG2_E = 1.4426950408889634
f32 = jnp.float32
bf16 = jnp.bfloat16

VMEM = pl.BlockSpec(memory_space=pltpu.VMEM)
SMEM = pl.BlockSpec(memory_space=pltpu.SMEM)
ANY = pl.BlockSpec(memory_space=pltpu.HBM)
MIB = 1024 * 1024


def shift_rep(a, by):
    return lax.ppermute(a, "rep", [(i, (i + by) % N_REP) for i in range(N_REP)])


def swap_core(a):
    return lax.ppermute(a, "c", [(0, 1), (1, 0)])


def cross_x(a, bits):
    return lax.ppermute(a, "x", [(i, i ^ bits) for i in range(N_X)])


def cross_z(a, bits):
    return lax.ppermute(a, "z", [(i, i ^ bits) for i in range(N_Z)])


def column(hot_ref, slot, rank, half):
    at = hot_ref[slot] % PER_DEV * BLK + rank * QUARTER + half * HALF
    return pl.ds(pl.multiple_of(at, HALF), HALF)


def run_copies(copies):
    for c in copies:
        c.start()
    for c in copies:
        c.wait()


def first_cut_kernel(hot_ref, lat_ref, up_ref, down_ref, sems):
    far = (lax.axis_index("rep") + 2) % N_REP
    copies = []
    for half, dst in enumerate((up_ref, down_ref)):
        for slot in range(HOT_GRP):
            copies.append(
                pltpu.make_async_copy(
                    lat_ref.at[:, column(hot_ref, slot, far, half)],
                    dst.at[:, pl.ds(slot * HALF, HALF)],
                    sems.at[len(copies)],
                )
            )
    run_copies(copies)


def own_cut_kernel(hot_ref, lat_ref, right_ref, left_ref, mine_ref, sems):
    rank = lax.axis_index("rep")
    copies = []
    for hop, dst in ((1, right_ref), (3, left_ref), (0, mine_ref)):
        for half in range(2):
            for slot in range(HOT_GRP):
                copies.append(
                    pltpu.make_async_copy(
                        lat_ref.at[:, column(hot_ref, slot, (rank + hop) % N_REP, half)],
                        dst.at[:, pl.ds(half * PAIR + slot * HALF, HALF)],
                        sems.at[len(copies)],
                    )
                )
    run_copies(copies)


def pass_on_kernel(hot_ref, from_left, from_right, right_in, left_in, right_ref, left_ref):
    rank = lax.axis_index("rep")
    right_ref[:, PAIR:] = right_in[:, PAIR:]
    left_ref[:, :PAIR] = left_in[:, :PAIR]
    for slot in range(HOT_GRP):
        a = slice(slot * HALF, (slot + 1) * HALF)
        b = slice(PAIR + slot * HALF, PAIR + (slot + 1) * HALF)
        here = hot_ref[slot] // PER_DEV == rank

        @pl.when(here)
        def _():
            right_ref[:, a] = right_in[:, a]
            left_ref[:, b] = left_in[:, b]

        @pl.when(jnp.logical_not(here))
        def _():
            right_ref[:, a] = from_left[:, a]
            left_ref[:, b] = from_right[:, a]


def settle_kernel(hot_ref, from_left, from_right, mine_in, mine_ref):
    rank = lax.axis_index("rep")
    for slot in range(HOT_GRP):
        a = slice(slot * HALF, (slot + 1) * HALF)
        b = slice(PAIR + slot * HALF, PAIR + (slot + 1) * HALF)
        away = (hot_ref[slot] // PER_DEV - rank + N_REP) % N_REP

        @pl.when(away == 0)
        def _():
            mine_ref[:, a] = mine_in[:, a]
            mine_ref[:, b] = mine_in[:, b]

        @pl.when(away >= 2)
        def _():
            mine_ref[:, a] = from_left[:, a]

        @pl.when(away == 1)
        def _():
            mine_ref[:, a] = from_right[:, a]

        @pl.when(away == 3)
        def _():
            mine_ref[:, b] = from_left[:, b]

        @pl.when((away == 1) | (away == 2))
        def _():
            mine_ref[:, b] = from_right[:, b]


def three_terms(v):
    hi = v.astype(bf16)
    mid = (v - hi.astype(f32)).astype(bf16)
    low = (v - hi.astype(f32) - mid.astype(f32)).astype(bf16)
    return [hi, mid, low]


def visible_lengths(len_ref, rows):
    count = len_ref.shape[0]
    line = lax.broadcasted_iota(jnp.int32, (count, 1), 0)
    lens = jnp.zeros((count, 1), jnp.int32)
    for i in range(count):
        lens = jnp.where(line == i, len_ref[i], lens)
    return jnp.concatenate([lens] * (rows // count), axis=0)


def row_numbers(hot_ref, other, away, half, halves):
    x, z, c = lax.axis_index("x"), lax.axis_index("z"), lax.axis_index("c")
    group = (x * N_Z + z) * N_C + c + other * (1 - 2 * c)
    at = (lax.axis_index("rep") + away) % N_REP * QUARTER
    lane = lax.broadcasted_iota(jnp.int32, (1, HALF), 1)
    return jnp.concatenate(
        [
            (group * BPG + hot_ref[slot]) * BLK + at + h * HALF + lane
            for h in range(half, half + halves)
            for slot in range(HOT_GRP)
        ],
        axis=1,
    )


NEAR = (0, 3, 1)
FAR = 2


def fold(op, s):
    return functools.reduce(op, [s[:, i : i + 128] for i in range(0, s.shape[1], 128)])


def score_kernel(other, len_ref, hot_ref, *refs):
    q_refs, key_refs, outs = refs[:N_X], refs[N_X : N_X + len(NEAR)], refs[N_X + len(NEAR) :]
    lens = visible_lengths(len_ref, q_refs[0].shape[0])
    rows = [row_numbers(hot_ref, other, away, 0, 2) for away in NEAR]
    for i, q_ref in enumerate(q_refs):
        s_ref, peak_ref = outs[2 * i : 2 * i + 2]
        q = q_ref[...]
        peaks = []
        for j, k_ref in enumerate(key_refs):
            s = jnp.dot(q, k_ref[...], preferred_element_type=f32)
            s = jnp.where(rows[j] < lens, s, NEVER)
            s_ref[:, j * CHUNK : (j + 1) * CHUNK] = s
            peaks.append(fold(jnp.maximum, s))
        peak_ref[...] = functools.reduce(jnp.maximum, peaks)


def attend_kernel(q_ref, *refs):
    n = len(NEAR)
    (s_refs, peak_refs), refs = (refs[0:4:2], refs[1:4:2]), refs[4:]
    (len_ref, *hot_refs), refs = refs[:3], refs[3:]
    key_refs, o_ref = refs[:-1], refs[-1]
    q = q_ref[...]
    lens = visible_lengths(len_ref, q.shape[0])
    last = []
    for other in range(N_C):
        for half in range(2):
            k_ref = key_refs[other * (n + 2) + n + half]
            rows = row_numbers(hot_refs[other], other, FAR, half, 1)
            s = jnp.dot(q, k_ref[...], preferred_element_type=f32)
            last.append(jnp.where(rows < lens, s, NEVER))
    parts = []
    for other in range(N_C):
        keys = key_refs[other * (n + 2) : (other + 1) * (n + 2)]
        scores = [s_refs[other][:, i * CHUNK : (i + 1) * CHUNK] for i in range(n)]
        scores += last[other * 2 : other * 2 + 2]
        peak = peak_refs[other][...]
        for s in last[other * 2 : other * 2 + 2]:
            peak = jnp.maximum(peak, fold(jnp.maximum, s))
        peak = peak.max(axis=1, keepdims=True)
        total = 0.0
        numer = None
        for s, k_ref in zip(scores, keys):
            w = jnp.exp2((s - peak) * (SCALE * LOG2_E)).astype(bf16)
            total = total + fold(jnp.add, w.astype(f32))
            v = lax.dot_general(
                w, k_ref[:LAT, :], (((1,), (1,)), ((), ())), preferred_element_type=f32
            )
            numer = v if numer is None else numer + v
        parts.append((peak, total.sum(axis=1, keepdims=True), numer))
    top = jnp.maximum(parts[0][0], parts[1][0])
    numer, total = 0.0, 0.0
    for peak, t, v in parts:
        f = jnp.where(peak > NEVER / 2, jnp.exp((peak - top) * SCALE), 0.0)
        numer = numer + v * f
        total = total + t * f
    o = (numer * (1.0 / jnp.maximum(total, 1.0))).astype(bf16)
    rows = q.shape[0]
    lanes = lax.broadcasted_iota(jnp.int32, (rows, 128), 1)
    stats = jnp.where(lanes == 0, top * SCALE, total).T[:2, :]
    terms = three_terms(stats[0:1]) + three_terms(stats[1:2])
    terms = [t.astype(f32) for t in terms] + [jnp.zeros((STAT_ROWS - 6, rows), f32)]
    o_ref[:rows, :] = o
    o_ref[rows:, :rows] = jnp.concatenate(terms, axis=0).astype(bf16)
    o_ref[rows:, rows:] = jnp.zeros((STAT_ROWS, LAT - rows), bf16)


def merge_kernel(*refs):
    parts, outs = refs[:N_X], refs[N_X:]
    rows = parts[0].shape[0] - STAT_ROWS
    tops, totals = [], []
    for p in parts:
        s = p[rows:, :rows].astype(f32)
        tops.append(s[0:1] + s[1:2] + s[2:3])
        totals.append(s[3:4] + s[4:5] + s[5:6])
    top = functools.reduce(jnp.maximum, tops)
    weights = [t * jnp.exp(m - top) for m, t in zip(tops, totals)]
    total = sum(weights)
    inv = 1.0 / jnp.maximum(total, 1.0)
    table = [w * inv for w in weights] + [top, total]
    table.append(jnp.zeros((128 - len(table), rows), f32))
    table = jnp.concatenate(table, axis=0).T
    n = rows // N_Z
    lane = lax.broadcasted_iota(jnp.int32, (n, 128), 1)
    for i, ref in enumerate(outs):
        at = slice(i * n, (i + 1) * n)
        acc = 0.0
        for j, p in enumerate(parts):
            acc = acc + p[at, :].astype(f32) * table[at, j : j + 1]
        ref[:, :LAT] = acc.astype(ref.dtype)
        packed = jnp.zeros((n, 128), f32)
        terms = three_terms(table[at, N_X : N_X + 1])
        terms += three_terms(table[at, N_X + 1 : N_X + 2])
        for j, term in enumerate(terms):
            packed = jnp.where(lane == j, term.astype(f32), packed)
        ref[:, LAT:] = packed.astype(ref.dtype)


def finish_kernel(*refs):
    parts, out_ref = [r[...].astype(f32) for r in refs[:-1]], refs[-1]
    tops, totals = [], []
    for p in parts:
        s = p[:, LAT:]
        tops.append(s[:, 0:1] + s[:, 1:2] + s[:, 2:3])
        totals.append(s[:, 3:4] + s[:, 4:5] + s[:, 5:6])
    top = functools.reduce(jnp.maximum, tops)
    weights = [t * jnp.exp(m - top) for m, t in zip(tops, totals)]
    o = sum(p[:, :LAT] * w for p, w in zip(parts, weights)) / sum(weights)
    count = out_ref.shape[0]
    for head in range(o.shape[0] // count):
        out_ref[:, head * LAT : (head + 1) * LAT] = o[head * count : (head + 1) * count].astype(bf16)


def call(kernel, outs, in_specs, args, mib=16, **more):
    return pl.pallas_call(
        kernel,
        out_shape=tuple(jax.ShapeDtypeStruct(*o) for o in outs),
        in_specs=in_specs,
        out_specs=(VMEM,) * len(outs),
        compiler_params=pltpu.CompilerParams(vmem_limit_bytes=mib * MIB),
        **more,
    )(*args)


def on_device(latents, queries, hot_ids, lengths):
    by_column = latents.T
    count = queries.shape[0]
    chunk, pair = ((WIDTH, CHUNK), bf16), ((WIDTH, PAIR), bf16)

    up, down = call(
        first_cut_kernel,
        [pair, pair],
        [SMEM, ANY],
        [hot_ids, by_column],
        mib=50,
        scratch_shapes=[pltpu.SemaphoreType.DMA((4,))],
    )
    own = queries.reshape(count, -1, WIDTH).transpose(1, 0, 2).reshape(-1, WIDTH)
    near = jnp.concatenate([own, cross_z(own, 4)], axis=0)
    up, down, near = lax.optimization_barrier((up, down, near))
    up, down = shift_rep(up, 1), shift_rep(down, -1)
    near = jnp.concatenate([near, cross_z(near, 2)], axis=0)
    right, left, mine = call(
        own_cut_kernel,
        [chunk] * 3,
        [SMEM, ANY],
        [hot_ids, by_column],
        mib=50,
        scratch_shapes=[pltpu.SemaphoreType.DMA((12,))],
    )
    up, down, near = lax.optimization_barrier((up, down, near))
    right, left = call(
        pass_on_kernel,
        [chunk] * 2,
        [SMEM] + [VMEM] * 4,
        [hot_ids, up, down, right, left],
    )
    from_left, from_right = shift_rep(right, 1), shift_rep(left, -1)
    near = jnp.concatenate([near, cross_z(near, 1)], axis=0)
    asked = [near] + [cross_x(near, bits) for bits in range(1, N_X)]
    from_left, from_right, asked[1], asked[3] = lax.optimization_barrier(
        (from_left, from_right, asked[1], asked[3])
    )
    (mine,) = call(
        settle_kernel,
        [chunk],
        [SMEM] + [VMEM] * 3,
        [hot_ids, from_left, from_right, mine],
    )
    hot_other = swap_core(hot_ids)

    of_left, of_right = shift_rep(mine, 1), shift_rep(mine, -1)
    of_left, of_right, asked[2] = lax.optimization_barrier((of_left, of_right, asked[2]))
    far_a, far_b = shift_rep(of_left[:, :PAIR], 1), shift_rep(of_right[:, PAIR:], -1)
    keys = [mine, of_left, of_right]
    swapped = [swap_core(k) for k in keys]
    asked, swapped = lax.optimization_barrier((asked, swapped))

    rows = near.shape[0]
    scores = []
    for other, (hot, some) in enumerate(((hot_ids, keys), (hot_other, swapped))):
        found = call(
            functools.partial(score_kernel, other),
            [((rows, len(NEAR) * CHUNK), f32), ((rows, 128), f32)] * N_X,
            [SMEM, SMEM] + [VMEM] * (N_X + len(NEAR)),
            [lengths, hot, *asked, *some],
        )
        scores.append([found[2 * hop : 2 * hop + 2] for hop in range(N_X)])
    scores, far_a, far_b = lax.optimization_barrier((scores, far_a, far_b))
    keys += [far_a, far_b]
    swapped += [swap_core(far_a), swap_core(far_b)]

    parts = []
    for i, hop in enumerate((1, 3, 2, 0)):
        if i > 1:
            lengths, parts[i - 2] = lax.optimization_barrier((lengths, parts[i - 2]))
        (o,) = call(
            attend_kernel,
            [((rows + STAT_ROWS, LAT), bf16)],
            [VMEM] * 5 + [SMEM] * 3 + [VMEM] * (N_C * len(keys)),
            [asked[hop], *scores[0][hop], *scores[1][hop], lengths, hot_ids, hot_other, *keys, *swapped],
        )
        lengths, o = lax.optimization_barrier((lengths, o))
        parts.append(cross_x(o, hop) if hop else o)

    n = own.shape[0]
    ours, *sends = call(
        merge_kernel,
        [((n, LAT + 128), f32 if i == 0 else bf16) for i in range(N_Z)],
        [VMEM] * N_X,
        parts,
    )
    sends = [cross_z(s, bits) for s, bits in zip(sends, Z_ORDER[1:])]
    (out,) = call(
        finish_kernel,
        [((count, n // count * LAT), bf16)],
        [VMEM] * N_Z,
        [ours, *sends],
    )
    return out


def solution(mesh):
    assert dict(mesh.shape) == {"ctx": N_X * N_Z * N_C, "rep": N_REP}
    split = Mesh(mesh.devices.reshape(N_X, N_Z, N_C, N_REP), ("x", "z", "c", "rep"))
    ctx = ("x", "z", "c")
    placed = (P((*ctx, "rep"), None), P("rep", ctx), P(ctx), P("rep"))
    return jax.shard_map(
        on_device, mesh=split, in_specs=placed, out_specs=P("rep", ctx), check_vma=False
    )
```

```python
import functools

import jax
import jax.numpy as jnp
from jax import lax
from jax.experimental import pallas as pl
from jax.experimental.pallas import tpu as pltpu
from jax.sharding import Mesh, PartitionSpec as P

H = 128
LAT = 512
ROPE = 64
QK = 192
BLK = 1024
HOT_GRP = 2
BPG = 16
WIDTH = LAT + ROPE
N_X = 4
N_Z = 8
N_C = 2
N_REP = 4
PER_DEV = BPG // N_REP
QUARTER = BLK // N_REP
HALF = QUARTER // 2
PAIR = HOT_GRP * HALF
CHUNK = 2 * PAIR
NEVER = -1e30
STAT_ROWS = 8
Z_ORDER = (0, 4, 2, 6, 1, 5, 3, 7)
SCALE = QK**-0.5
LOG2_E = 1.4426950408889634
N_FAR = N_Z // 2
f32 = jnp.float32
bf16 = jnp.bfloat16

VMEM = pl.BlockSpec(memory_space=pltpu.VMEM)
SMEM = pl.BlockSpec(memory_space=pltpu.SMEM)
ANY = pl.BlockSpec(memory_space=pltpu.HBM)
MIB = 1024 * 1024


def shift_rep(a, by):
    return lax.ppermute(a, "rep", [(i, (i + by) % N_REP) for i in range(N_REP)])


def swap_core(a):
    return lax.ppermute(a, "c", [(0, 1), (1, 0)])


def cross_x(a, bits):
    return lax.ppermute(a, "x", [(i, i ^ bits) for i in range(N_X)])


def cross_z(a, bits):
    return lax.ppermute(a, "z", [(i, i ^ bits) for i in range(N_Z)])


def column(hot_ref, slot, rank, half):
    at = hot_ref[slot] % PER_DEV * BLK + rank * QUARTER + half * HALF
    return pl.ds(pl.multiple_of(at, HALF), HALF)


def run_copies(copies):
    for c in copies:
        c.start()
    for c in copies:
        c.wait()


def first_cut_kernel(hot_ref, lat_ref, up_ref, down_ref, sems):
    far = (lax.axis_index("rep") + 2) % N_REP
    copies = []
    for half, dst in enumerate((up_ref, down_ref)):
        for slot in range(HOT_GRP):
            copies.append(
                pltpu.make_async_copy(
                    lat_ref.at[:, column(hot_ref, slot, far, half)],
                    dst.at[:, pl.ds(slot * HALF, HALF)],
                    sems.at[len(copies)],
                )
            )
    run_copies(copies)


def own_cut_kernel(hot_ref, lat_ref, right_a, right_b, left_a, left_b, mine_ref, sems):
    rank = lax.axis_index("rep")
    copies = []
    for hop, halves in ((1, (right_a, right_b)), (3, (left_a, left_b)), (0, (mine_ref, mine_ref))):
        for half, dst in enumerate(halves):
            for slot in range(HOT_GRP):
                to = slot * HALF + (half * PAIR if hop == 0 else 0)
                copies.append(
                    pltpu.make_async_copy(
                        lat_ref.at[:, column(hot_ref, slot, (rank + hop) % N_REP, half)],
                        dst.at[:, pl.ds(to, HALF)],
                        sems.at[len(copies)],
                    )
                )
    run_copies(copies)


def pass_on_kernel(hot_ref, from_left, from_right, right_in, left_in, right_ref, left_ref):
    rank = lax.axis_index("rep")
    for slot in range(HOT_GRP):
        a = slice(slot * HALF, (slot + 1) * HALF)
        here = hot_ref[slot] // PER_DEV == rank

        @pl.when(here)
        def _():
            right_ref[:, a] = right_in[:, a]
            left_ref[:, a] = left_in[:, a]

        @pl.when(jnp.logical_not(here))
        def _():
            right_ref[:, a] = from_left[:, a]
            left_ref[:, a] = from_right[:, a]


def settle_kernel(hot_ref, left_a, left_b, right_a, right_b, mine_in, mine_ref):
    rank = lax.axis_index("rep")
    for slot in range(HOT_GRP):
        a = slice(slot * HALF, (slot + 1) * HALF)
        b = slice(PAIR + slot * HALF, PAIR + (slot + 1) * HALF)
        away = (hot_ref[slot] // PER_DEV - rank + N_REP) % N_REP

        @pl.when(away == 0)
        def _():
            mine_ref[:, a] = mine_in[:, a]
            mine_ref[:, b] = mine_in[:, b]

        @pl.when(away >= 2)
        def _():
            mine_ref[:, a] = left_a[:, a]

        @pl.when(away == 1)
        def _():
            mine_ref[:, a] = right_a[:, a]

        @pl.when(away == 3)
        def _():
            mine_ref[:, b] = left_b[:, a]

        @pl.when((away == 1) | (away == 2))
        def _():
            mine_ref[:, b] = right_b[:, a]


def three_terms(v):
    hi = v.astype(bf16)
    mid = (v - hi.astype(f32)).astype(bf16)
    low = (v - hi.astype(f32) - mid.astype(f32)).astype(bf16)
    return [hi, mid, low]


def visible_lengths(len_ref, rows):
    count = len_ref.shape[0]
    line = lax.broadcasted_iota(jnp.int32, (count, 1), 0)
    lens = jnp.zeros((count, 1), jnp.int32)
    for i in range(count):
        lens = jnp.where(line == i, len_ref[i], lens)
    return jnp.concatenate([lens] * (rows // count), axis=0)


def row_numbers(hot_ref, other, away, half, halves):
    x, z, c = lax.axis_index("x"), lax.axis_index("z"), lax.axis_index("c")
    group = (x * N_Z + z) * N_C + c + other * (1 - 2 * c)
    at = (lax.axis_index("rep") + away) % N_REP * QUARTER
    lane = lax.broadcasted_iota(jnp.int32, (1, HALF), 1)
    return jnp.concatenate(
        [
            (group * BPG + hot_ref[slot]) * BLK + at + h * HALF + lane
            for h in range(half, half + halves)
            for slot in range(HOT_GRP)
        ],
        axis=1,
    )


PLACES = ((0, 0, 2), (3, 0, 2), (1, 0, 2), (2, 0, 1), (2, 1, 1))


def fold(op, s):
    return functools.reduce(op, [s[:, i : i + 128] for i in range(0, s.shape[1], 128)])


def attend_kernel(q_ref, len_ref, hot_ref, hot_other_ref, *refs):
    n = len(PLACES)
    key_refs, o_ref = refs[:-1], refs[-1]
    q = q_ref[...]
    lens = visible_lengths(len_ref, q.shape[0])
    parts = []
    for other, hot in enumerate((hot_ref, hot_other_ref)):
        keys = key_refs[other * n : (other + 1) * n]
        scores = []
        for k_ref, place in zip(keys, PLACES):
            numbers = row_numbers(hot, other, *place)
            s = jnp.dot(q, k_ref[...], preferred_element_type=f32)
            scores.append(jnp.where(numbers < lens, s, NEVER))
        peak = functools.reduce(jnp.maximum, [fold(jnp.maximum, s) for s in scores])
        peak = peak.max(axis=1, keepdims=True)
        total = 0.0
        numer = None
        for s, k_ref in zip(scores, keys):
            w = jnp.exp2((s - peak) * (SCALE * LOG2_E)).astype(bf16)
            total = total + fold(jnp.add, w.astype(f32))
            v = lax.dot_general(
                w, k_ref[:LAT, :], (((1,), (1,)), ((), ())), preferred_element_type=f32
            )
            numer = v if numer is None else numer + v
        parts.append((peak, total.sum(axis=1, keepdims=True), numer))
    top = jnp.maximum(parts[0][0], parts[1][0])
    numer, total = 0.0, 0.0
    for peak, t, v in parts:
        f = jnp.where(peak > NEVER / 2, jnp.exp((peak - top) * SCALE), 0.0)
        numer = numer + v * f
        total = total + t * f
    o = (numer * (1.0 / jnp.maximum(total, 1.0))).astype(bf16)
    rows = q.shape[0]
    lanes = lax.broadcasted_iota(jnp.int32, (rows, 128), 1)
    stats = jnp.where(lanes == 0, top * SCALE, total).T[:2, :]
    terms = three_terms(stats[0:1]) + three_terms(stats[1:2])
    terms = [t.astype(f32) for t in terms] + [jnp.zeros((STAT_ROWS - 6, rows), f32)]
    o_ref[:rows, :] = o
    o_ref[rows:, :rows] = jnp.concatenate(terms, axis=0).astype(bf16)
    o_ref[rows:, rows:] = jnp.zeros((STAT_ROWS, LAT - rows), bf16)


def merge_kernel(*refs):
    parts, outs = refs[:N_X], refs[N_X:]
    rows = parts[0].shape[0] - STAT_ROWS
    tops, totals = [], []
    for p in parts:
        s = p[rows:, :rows].astype(f32)
        tops.append(s[0:1] + s[1:2] + s[2:3])
        totals.append(s[3:4] + s[4:5] + s[5:6])
    top = functools.reduce(jnp.maximum, tops)
    weights = [t * jnp.exp(m - top) for m, t in zip(tops, totals)]
    total = sum(weights)
    inv = 1.0 / jnp.maximum(total, 1.0)
    table = [w * inv for w in weights] + [top, total]
    table.append(jnp.zeros((128 - len(table), rows), f32))
    table = jnp.concatenate(table, axis=0).T
    n = rows // N_Z
    lane = lax.broadcasted_iota(jnp.int32, (n, 128), 1)
    for i, ref in enumerate(outs):
        at = slice(i * n, (i + 1) * n)
        acc = 0.0
        for j, p in enumerate(parts):
            acc = acc + p[at, :].astype(f32) * table[at, j : j + 1]
        ref[:, :LAT] = acc.astype(ref.dtype)
        packed = jnp.zeros((n, 128), f32)
        terms = three_terms(table[at, N_X : N_X + 1])
        terms += three_terms(table[at, N_X + 1 : N_X + 2])
        for j, term in enumerate(terms):
            packed = jnp.where(lane == j, term.astype(f32), packed)
        ref[:, LAT:] = packed.astype(ref.dtype)


def finish_kernel(*refs):
    parts, out_ref = [r[...].astype(f32) for r in refs[:-1]], refs[-1]
    tops, totals = [], []
    for p in parts:
        s = p[:, LAT:]
        tops.append(s[:, 0:1] + s[:, 1:2] + s[:, 2:3])
        totals.append(s[:, 3:4] + s[:, 4:5] + s[:, 5:6])
    top = functools.reduce(jnp.maximum, tops)
    weights = [t * jnp.exp(m - top) for m, t in zip(tops, totals)]
    o = sum(p[:, :LAT] * w for p, w in zip(parts, weights)) / sum(weights)
    count = out_ref.shape[0]
    for head in range(o.shape[0] // count):
        out_ref[:, head * LAT : (head + 1) * LAT] = o[head * count : (head + 1) * count].astype(bf16)


def call(kernel, outs, in_specs, args, mib=16, **more):
    return pl.pallas_call(
        kernel,
        out_shape=tuple(jax.ShapeDtypeStruct(*o) for o in outs),
        in_specs=in_specs,
        out_specs=(VMEM,) * len(outs),
        compiler_params=pltpu.CompilerParams(vmem_limit_bytes=mib * MIB),
        **more,
    )(*args)


def on_device(latents, queries, hot_ids, lengths):
    by_column = latents.T
    count = queries.shape[0]
    chunk, pair = ((WIDTH, CHUNK), bf16), ((WIDTH, PAIR), bf16)

    up, down = call(
        first_cut_kernel,
        [pair, pair],
        [SMEM, ANY],
        [hot_ids, by_column],
        mib=50,
        scratch_shapes=[pltpu.SemaphoreType.DMA((4,))],
    )
    up, down = shift_rep(up, 1), shift_rep(down, -1)
    own = queries.reshape(count, -1, WIDTH).transpose(1, 0, 2).reshape(-1, WIDTH)
    near = jnp.concatenate([own, cross_z(own, 4)], axis=0)
    hot_other = swap_core(hot_ids)
    right_a, right_b, left_a, left_b, mine = call(
        own_cut_kernel,
        [pair] * 4 + [chunk],
        [SMEM, ANY],
        [hot_ids, by_column],
        mib=50,
        scratch_shapes=[pltpu.SemaphoreType.DMA((12,))],
    )
    from_left_b, from_right_a = shift_rep(right_b, 1), shift_rep(left_a, -1)
    up, down, near, hot_other = lax.optimization_barrier((up, down, near, hot_other))
    right_a, left_b = call(
        pass_on_kernel,
        [pair] * 2,
        [SMEM] + [VMEM] * 4,
        [hot_ids, up, down, right_a, left_b],
    )
    from_left_a, from_right_b = shift_rep(right_a, 1), shift_rep(left_b, -1)
    for bits in (2, 1):
        near = jnp.concatenate([near, cross_z(near, bits)], axis=0)
    (mine,) = call(
        settle_kernel,
        [chunk],
        [SMEM] + [VMEM] * 5,
        [hot_ids, from_left_a, from_left_b, from_right_a, from_right_b, mine],
    )
    own_quarter, near = lax.optimization_barrier((mine, near))
    asked = [near] + [cross_x(near, bits) for bits in range(1, N_X)]

    of_left, of_right, swapped = shift_rep(mine, 1), shift_rep(mine, -1), swap_core(own_quarter)
    of_left, of_right, swapped = lax.optimization_barrier((of_left, of_right, swapped))
    far_a, far_b = shift_rep(of_left[:, :PAIR], 1), shift_rep(of_right[:, PAIR:], -1)
    far_a, far_b, *asked = lax.optimization_barrier((far_a, far_b, *asked))
    keys = [mine, of_left, of_right, far_a, far_b]
    keys = keys + [swapped] + [swap_core(k) for k in keys[1:]]

    rows = near.shape[0]
    parts = []
    for i, hop in enumerate((2, 1, 3, 0)):
        if i > 1:
            lengths, parts[i - 2] = lax.optimization_barrier((lengths, parts[i - 2]))
        (o,) = call(
            attend_kernel,
            [((rows + STAT_ROWS, LAT), bf16)],
            [VMEM, SMEM, SMEM, SMEM] + [VMEM] * len(keys),
            [asked[hop], lengths, hot_ids, hot_other, *keys],
        )
        lengths, o = lax.optimization_barrier((lengths, o))
        parts.append(cross_x(o, hop) if hop else o)

    n = own.shape[0]
    ours, *sends = call(
        merge_kernel,
        [((n, LAT + 128), f32 if i == 0 else bf16) for i in range(N_Z)],
        [VMEM] * N_X,
        parts,
    )
    sends = [cross_z(s, bits) for s, bits in zip(sends, Z_ORDER[1:])]
    (out,) = call(
        finish_kernel,
        [((count, n // count * LAT), bf16)],
        [VMEM] * N_Z,
        [ours, *sends],
    )
    return out


def solution(mesh):
    assert dict(mesh.shape) == {"ctx": N_X * N_Z * N_C, "rep": N_REP}
    split = Mesh(mesh.devices.reshape(N_X, N_Z, N_C, N_REP), ("x", "z", "c", "rep"))
    ctx = ("x", "z", "c")
    placed = (P((*ctx, "rep"), None), P("rep", ctx), P(ctx), P("rep"))
    return jax.shard_map(
        on_device, mesh=split, in_specs=placed, out_specs=P("rep", ctx), check_vma=False
    )
```

```python
import functools

import jax
import jax.numpy as jnp
from jax import lax
from jax.experimental import pallas as pl
from jax.experimental.pallas import tpu as pltpu
from jax.sharding import Mesh, PartitionSpec as P

H = 128
LAT = 512
ROPE = 64
QK = 192
BLK = 1024
HOT_GRP = 2
BPG = 16
WIDTH = LAT + ROPE
N_X = 4
N_Z = 8
N_C = 2
N_REP = 4
PER_DEV = BPG // N_REP
QUARTER = BLK // N_REP
HALF = QUARTER // 2
PAIR = HOT_GRP * HALF
CHUNK = 2 * PAIR
NEVER = -1e30
STAT_ROWS = 8
Z_ORDER = (0, 4, 2, 6, 1, 5, 3, 7)
SCALE = QK**-0.5
LOG2_E = 1.4426950408889634
N_FAR = N_Z // 2
f32 = jnp.float32
bf16 = jnp.bfloat16

VMEM = pl.BlockSpec(memory_space=pltpu.VMEM)
SMEM = pl.BlockSpec(memory_space=pltpu.SMEM)
ANY = pl.BlockSpec(memory_space=pltpu.HBM)
MIB = 1024 * 1024


def shift_rep(a, by):
    return lax.ppermute(a, "rep", [(i, (i + by) % N_REP) for i in range(N_REP)])


def swap_core(a):
    return lax.ppermute(a, "c", [(0, 1), (1, 0)])


def cross_x(a, bits):
    return lax.ppermute(a, "x", [(i, i ^ bits) for i in range(N_X)])


def cross_z(a, bits):
    return lax.ppermute(a, "z", [(i, i ^ bits) for i in range(N_Z)])


def column(hot_ref, slot, rank, half):
    at = hot_ref[slot] % PER_DEV * BLK + rank * QUARTER + half * HALF
    return pl.ds(pl.multiple_of(at, HALF), HALF)


def run_copies(copies):
    for c in copies:
        c.start()
    for c in copies:
        c.wait()


def first_cut_kernel(hot_ref, lat_ref, up_ref, down_ref, sems):
    far = (lax.axis_index("rep") + 2) % N_REP
    copies = []
    for half, dst in enumerate((up_ref, down_ref)):
        for slot in range(HOT_GRP):
            copies.append(
                pltpu.make_async_copy(
                    lat_ref.at[:, column(hot_ref, slot, far, half)],
                    dst.at[:, pl.ds(slot * HALF, HALF)],
                    sems.at[len(copies)],
                )
            )
    run_copies(copies)


def own_cut_kernel(hot_ref, lat_ref, right_a, right_b, left_a, left_b, mine_ref, sems):
    rank = lax.axis_index("rep")
    copies = []
    for hop, halves in ((1, (right_a, right_b)), (3, (left_a, left_b)), (0, (mine_ref, mine_ref))):
        for half, dst in enumerate(halves):
            for slot in range(HOT_GRP):
                to = slot * HALF + (half * PAIR if hop == 0 else 0)
                copies.append(
                    pltpu.make_async_copy(
                        lat_ref.at[:, column(hot_ref, slot, (rank + hop) % N_REP, half)],
                        dst.at[:, pl.ds(to, HALF)],
                        sems.at[len(copies)],
                    )
                )
    run_copies(copies)


def pass_on_kernel(hot_ref, from_left, from_right, right_in, left_in, right_ref, left_ref):
    rank = lax.axis_index("rep")
    for slot in range(HOT_GRP):
        a = slice(slot * HALF, (slot + 1) * HALF)
        here = hot_ref[slot] // PER_DEV == rank

        @pl.when(here)
        def _():
            right_ref[:, a] = right_in[:, a]
            left_ref[:, a] = left_in[:, a]

        @pl.when(jnp.logical_not(here))
        def _():
            right_ref[:, a] = from_left[:, a]
            left_ref[:, a] = from_right[:, a]


def settle_kernel(hot_ref, left_a, left_b, right_a, right_b, mine_in, mine_ref):
    rank = lax.axis_index("rep")
    for slot in range(HOT_GRP):
        a = slice(slot * HALF, (slot + 1) * HALF)
        b = slice(PAIR + slot * HALF, PAIR + (slot + 1) * HALF)
        away = (hot_ref[slot] // PER_DEV - rank + N_REP) % N_REP

        @pl.when(away == 0)
        def _():
            mine_ref[:, a] = mine_in[:, a]
            mine_ref[:, b] = mine_in[:, b]

        @pl.when(away >= 2)
        def _():
            mine_ref[:, a] = left_a[:, a]

        @pl.when(away == 1)
        def _():
            mine_ref[:, a] = right_a[:, a]

        @pl.when(away == 3)
        def _():
            mine_ref[:, b] = left_b[:, a]

        @pl.when((away == 1) | (away == 2))
        def _():
            mine_ref[:, b] = right_b[:, a]


def three_terms(v):
    hi = v.astype(bf16)
    mid = (v - hi.astype(f32)).astype(bf16)
    low = (v - hi.astype(f32) - mid.astype(f32)).astype(bf16)
    return [hi, mid, low]


def visible_lengths(len_ref, rows):
    count = len_ref.shape[0]
    line = lax.broadcasted_iota(jnp.int32, (count, 1), 0)
    lens = jnp.zeros((count, 1), jnp.int32)
    for i in range(count):
        lens = jnp.where(line == i, len_ref[i], lens)
    return jnp.concatenate([lens] * (rows // count), axis=0)


def row_numbers(hot_ref, other, away, half, halves):
    x, z, c = lax.axis_index("x"), lax.axis_index("z"), lax.axis_index("c")
    group = (x * N_Z + z) * N_C + c + other * (1 - 2 * c)
    at = (lax.axis_index("rep") + away) % N_REP * QUARTER
    lane = lax.broadcasted_iota(jnp.int32, (1, HALF), 1)
    return jnp.concatenate(
        [
            (group * BPG + hot_ref[slot]) * BLK + at + h * HALF + lane
            for h in range(half, half + halves)
            for slot in range(HOT_GRP)
        ],
        axis=1,
    )


PLACES = ((0, 0, 2), (3, 0, 2), (1, 0, 2), (2, 0, 1), (2, 1, 1))


def fold(op, s):
    return functools.reduce(op, [s[:, i : i + 128] for i in range(0, s.shape[1], 128)])


def attend_kernel(q_ref, len_ref, hot_ref, hot_other_ref, *refs):
    n = len(PLACES)
    key_refs, o_ref = refs[:-1], refs[-1]
    q = q_ref[...]
    lens = visible_lengths(len_ref, q.shape[0])
    parts = []
    for other, hot in enumerate((hot_ref, hot_other_ref)):
        keys = key_refs[other * n : (other + 1) * n]
        scores = []
        for k_ref, place in zip(keys, PLACES):
            numbers = row_numbers(hot, other, *place)
            s = jnp.dot(q, k_ref[...], preferred_element_type=f32)
            scores.append(jnp.where(numbers < lens, s, NEVER))
        peak = functools.reduce(jnp.maximum, [fold(jnp.maximum, s) for s in scores])
        peak = peak.max(axis=1, keepdims=True)
        total = 0.0
        numer = None
        for s, k_ref in zip(scores, keys):
            w = jnp.exp2((s - peak) * (SCALE * LOG2_E)).astype(bf16)
            total = total + fold(jnp.add, w.astype(f32))
            v = lax.dot_general(
                w, k_ref[:LAT, :], (((1,), (1,)), ((), ())), preferred_element_type=f32
            )
            numer = v if numer is None else numer + v
        parts.append((peak, total.sum(axis=1, keepdims=True), numer))
    top = jnp.maximum(parts[0][0], parts[1][0])
    numer, total = 0.0, 0.0
    for peak, t, v in parts:
        f = jnp.where(peak > NEVER / 2, jnp.exp((peak - top) * SCALE), 0.0)
        numer = numer + v * f
        total = total + t * f
    o = (numer * (1.0 / jnp.maximum(total, 1.0))).astype(bf16)
    rows = q.shape[0]
    lanes = lax.broadcasted_iota(jnp.int32, (rows, 128), 1)
    stats = jnp.where(lanes == 0, top * SCALE, total).T[:2, :]
    terms = three_terms(stats[0:1]) + three_terms(stats[1:2])
    terms = [t.astype(f32) for t in terms] + [jnp.zeros((STAT_ROWS - 6, rows), f32)]
    o_ref[:rows, :] = o
    o_ref[rows:, :rows] = jnp.concatenate(terms, axis=0).astype(bf16)
    o_ref[rows:, rows:] = jnp.zeros((STAT_ROWS, LAT - rows), bf16)


def merge_kernel(*refs):
    parts, outs = refs[:N_X], refs[N_X:]
    rows = parts[0].shape[0] - STAT_ROWS
    tops, totals = [], []
    for p in parts:
        s = p[rows:, :rows].astype(f32)
        tops.append(s[0:1] + s[1:2] + s[2:3])
        totals.append(s[3:4] + s[4:5] + s[5:6])
    top = functools.reduce(jnp.maximum, tops)
    weights = [t * jnp.exp(m - top) for m, t in zip(tops, totals)]
    total = sum(weights)
    inv = 1.0 / jnp.maximum(total, 1.0)
    table = [w * inv for w in weights] + [top, total]
    table.append(jnp.zeros((128 - len(table), rows), f32))
    table = jnp.concatenate(table, axis=0).T
    n = rows // N_Z
    lane = lax.broadcasted_iota(jnp.int32, (n, 128), 1)
    for i, ref in enumerate(outs):
        at = slice(i * n, (i + 1) * n)
        acc = 0.0
        for j, p in enumerate(parts):
            acc = acc + p[at, :].astype(f32) * table[at, j : j + 1]
        ref[:, :LAT] = acc.astype(ref.dtype)
        packed = jnp.zeros((n, 128), f32)
        terms = three_terms(table[at, N_X : N_X + 1])
        terms += three_terms(table[at, N_X + 1 : N_X + 2])
        for j, term in enumerate(terms):
            packed = jnp.where(lane == j, term.astype(f32), packed)
        ref[:, LAT:] = packed.astype(ref.dtype)


def finish_kernel(*refs):
    parts, out_ref = [r[...].astype(f32) for r in refs[:-1]], refs[-1]
    tops, totals = [], []
    for p in parts:
        s = p[:, LAT:]
        tops.append(s[:, 0:1] + s[:, 1:2] + s[:, 2:3])
        totals.append(s[:, 3:4] + s[:, 4:5] + s[:, 5:6])
    top = functools.reduce(jnp.maximum, tops)
    weights = [t * jnp.exp(m - top) for m, t in zip(tops, totals)]
    o = sum(p[:, :LAT] * w for p, w in zip(parts, weights)) / sum(weights)
    count = out_ref.shape[0]
    for head in range(o.shape[0] // count):
        out_ref[:, head * LAT : (head + 1) * LAT] = o[head * count : (head + 1) * count].astype(bf16)


def call(kernel, outs, in_specs, args, mib=16, **more):
    return pl.pallas_call(
        kernel,
        out_shape=tuple(jax.ShapeDtypeStruct(*o) for o in outs),
        in_specs=in_specs,
        out_specs=(VMEM,) * len(outs),
        compiler_params=pltpu.CompilerParams(vmem_limit_bytes=mib * MIB),
        **more,
    )(*args)


def on_device(latents, queries, hot_ids, lengths):
    by_column = latents.T
    count = queries.shape[0]
    chunk, pair = ((WIDTH, CHUNK), bf16), ((WIDTH, PAIR), bf16)

    up, down = call(
        first_cut_kernel,
        [pair, pair],
        [SMEM, ANY],
        [hot_ids, by_column],
        mib=50,
        scratch_shapes=[pltpu.SemaphoreType.DMA((4,))],
    )
    up, down = shift_rep(up, 1), shift_rep(down, -1)
    own = queries.reshape(count, -1, WIDTH).transpose(1, 0, 2).reshape(-1, WIDTH)
    near = jnp.concatenate([own, cross_z(own, 4)], axis=0)
    hot_other = swap_core(hot_ids)
    right_a, right_b, left_a, left_b, mine = call(
        own_cut_kernel,
        [pair] * 4 + [chunk],
        [SMEM, ANY],
        [hot_ids, by_column],
        mib=50,
        scratch_shapes=[pltpu.SemaphoreType.DMA((12,))],
    )
    from_left_b, from_right_a = shift_rep(right_b, 1), shift_rep(left_a, -1)
    up, down, near, hot_other = lax.optimization_barrier((up, down, near, hot_other))
    right_a, left_b = call(
        pass_on_kernel,
        [pair] * 2,
        [SMEM] + [VMEM] * 4,
        [hot_ids, up, down, right_a, left_b],
    )
    from_left_a, from_right_b = shift_rep(right_a, 1), shift_rep(left_b, -1)
    for bits in (2, 1):
        near = jnp.concatenate([near, cross_z(near, bits)], axis=0)
    (mine,) = call(
        settle_kernel,
        [chunk],
        [SMEM] + [VMEM] * 5,
        [hot_ids, from_left_a, from_left_b, from_right_a, from_right_b, mine],
    )
    asked = [near] + [cross_x(near, bits) for bits in range(1, N_X)]

    of_left, of_right = shift_rep(mine, 1), shift_rep(mine, -1)
    far_a, far_b = shift_rep(of_left[:, :PAIR], 1), shift_rep(of_right[:, PAIR:], -1)
    far_a, far_b, *asked = lax.optimization_barrier((far_a, far_b, *asked))
    keys = [mine, of_left, of_right, far_a, far_b]
    keys = keys + [swap_core(k) for k in keys]

    rows = near.shape[0]
    parts = []
    for i, hop in enumerate((2, 1, 3, 0)):
        if i > 1:
            lengths, parts[i - 2] = lax.optimization_barrier((lengths, parts[i - 2]))
        (o,) = call(
            attend_kernel,
            [((rows + STAT_ROWS, LAT), bf16)],
            [VMEM, SMEM, SMEM, SMEM] + [VMEM] * len(keys),
            [asked[hop], lengths, hot_ids, hot_other, *keys],
        )
        lengths, o = lax.optimization_barrier((lengths, o))
        parts.append(cross_x(o, hop) if hop else o)

    n = own.shape[0]
    ours, *sends = call(
        merge_kernel,
        [((n, LAT + 128), f32 if i == 0 else bf16) for i in range(N_Z)],
        [VMEM] * N_X,
        parts,
    )
    sends = [cross_z(s, bits) for s, bits in zip(sends, Z_ORDER[1:])]
    (out,) = call(
        finish_kernel,
        [((count, n // count * LAT), bf16)],
        [VMEM] * N_Z,
        [ours, *sends],
    )
    return out


def solution(mesh):
    assert dict(mesh.shape) == {"ctx": N_X * N_Z * N_C, "rep": N_REP}
    split = Mesh(mesh.devices.reshape(N_X, N_Z, N_C, N_REP), ("x", "z", "c", "rep"))
    ctx = ("x", "z", "c")
    placed = (P((*ctx, "rep"), None), P("rep", ctx), P(ctx), P("rep"))
    return jax.shard_map(
        on_device, mesh=split, in_specs=placed, out_specs=P("rep", ctx), check_vma=False
    )
```

```python
import functools

import jax
import jax.numpy as jnp
from jax import lax
from jax.experimental import pallas as pl
from jax.experimental.pallas import tpu as pltpu
from jax.sharding import Mesh, PartitionSpec as P

H = 128
LAT = 512
ROPE = 64
QK = 192
BLK = 1024
HOT_GRP = 2
BPG = 16
WIDTH = LAT + ROPE
N_X = 4
N_Z = 8
N_C = 2
N_REP = 4
PER_DEV = BPG // N_REP
QUARTER = BLK // N_REP
HALF = QUARTER // 2
PAIR = HOT_GRP * HALF
CHUNK = 2 * PAIR
NEVER = -1e30
N_FAR = N_Z // 2
STAT_ROWS = 8
Z_ORDER = (0, 4, 2, 6)
SCALE = QK**-0.5
LOG2_E = 1.4426950408889634
N_FAR = N_Z // 2
f32 = jnp.float32
bf16 = jnp.bfloat16

VMEM = pl.BlockSpec(memory_space=pltpu.VMEM)
SMEM = pl.BlockSpec(memory_space=pltpu.SMEM)
ANY = pl.BlockSpec(memory_space=pltpu.HBM)
MIB = 1024 * 1024


def shift_rep(a, by):
    return lax.ppermute(a, "rep", [(i, (i + by) % N_REP) for i in range(N_REP)])


def swap_core(a):
    return lax.ppermute(a, "c", [(0, 1), (1, 0)])


def cross_x(a, bits):
    return lax.ppermute(a, "x", [(i, i ^ bits) for i in range(N_X)])


def cross_xz(a, bits_x, bits_z):
    pairs = []
    for x in range(N_X):
        for z in range(N_Z):
            pairs.append((x * N_Z + z, (x ^ bits_x) * N_Z + (z ^ bits_z)))
    return lax.ppermute(a, ("x", "z"), pairs)


def cross_z(a, bits):
    return lax.ppermute(a, "z", [(i, i ^ bits) for i in range(N_Z)])


def column(hot_ref, slot, rank, half):
    at = hot_ref[slot] % PER_DEV * BLK + rank * QUARTER + half * HALF
    return pl.ds(pl.multiple_of(at, HALF), HALF)


def run_copies(copies):
    for c in copies:
        c.start()
    for c in copies:
        c.wait()


def first_cut_kernel(hot_ref, lat_ref, up_ref, down_ref, sems):
    far = (lax.axis_index("rep") + 2) % N_REP
    copies = []
    for half, dst in enumerate((up_ref, down_ref)):
        for slot in range(HOT_GRP):
            copies.append(
                pltpu.make_async_copy(
                    lat_ref.at[:, column(hot_ref, slot, far, half)],
                    dst.at[:, pl.ds(slot * HALF, HALF)],
                    sems.at[len(copies)],
                )
            )
    run_copies(copies)


def own_cut_kernel(hot_ref, lat_ref, right_a, right_b, left_a, left_b, mine_ref, sems):
    rank = lax.axis_index("rep")
    copies = []
    for hop, halves in ((1, (right_a, right_b)), (3, (left_a, left_b)), (0, (mine_ref, mine_ref))):
        for half, dst in enumerate(halves):
            for slot in range(HOT_GRP):
                to = slot * HALF + (half * PAIR if hop == 0 else 0)
                copies.append(
                    pltpu.make_async_copy(
                        lat_ref.at[:, column(hot_ref, slot, (rank + hop) % N_REP, half)],
                        dst.at[:, pl.ds(to, HALF)],
                        sems.at[len(copies)],
                    )
                )
    run_copies(copies)


def pass_on_kernel(hot_ref, from_left, from_right, right_in, left_in, right_ref, left_ref):
    rank = lax.axis_index("rep")
    for slot in range(HOT_GRP):
        a = slice(slot * HALF, (slot + 1) * HALF)
        here = hot_ref[slot] // PER_DEV == rank

        @pl.when(here)
        def _():
            right_ref[:, a] = right_in[:, a]
            left_ref[:, a] = left_in[:, a]

        @pl.when(jnp.logical_not(here))
        def _():
            right_ref[:, a] = from_left[:, a]
            left_ref[:, a] = from_right[:, a]


def settle_kernel(hot_ref, left_a, left_b, right_a, right_b, mine_in, mine_ref):
    rank = lax.axis_index("rep")
    for slot in range(HOT_GRP):
        a = slice(slot * HALF, (slot + 1) * HALF)
        b = slice(PAIR + slot * HALF, PAIR + (slot + 1) * HALF)
        away = (hot_ref[slot] // PER_DEV - rank + N_REP) % N_REP

        @pl.when(away == 0)
        def _():
            mine_ref[:, a] = mine_in[:, a]
            mine_ref[:, b] = mine_in[:, b]

        @pl.when(away >= 2)
        def _():
            mine_ref[:, a] = left_a[:, a]

        @pl.when(away == 1)
        def _():
            mine_ref[:, a] = right_a[:, a]

        @pl.when(away == 3)
        def _():
            mine_ref[:, b] = left_b[:, a]

        @pl.when((away == 1) | (away == 2))
        def _():
            mine_ref[:, b] = right_b[:, a]


def three_terms(v):
    hi = v.astype(bf16)
    mid = (v - hi.astype(f32)).astype(bf16)
    low = (v - hi.astype(f32) - mid.astype(f32)).astype(bf16)
    return [hi, mid, low]


def visible_lengths(len_ref, rows):
    count = len_ref.shape[0]
    line = lax.broadcasted_iota(jnp.int32, (count, 1), 0)
    lens = jnp.zeros((count, 1), jnp.int32)
    for i in range(count):
        lens = jnp.where(line == i, len_ref[i], lens)
    return jnp.concatenate([lens] * (rows // count), axis=0)


def row_numbers(hot_ref, other, away, half, halves):
    x, z, c = lax.axis_index("x"), lax.axis_index("z"), lax.axis_index("c")
    group = (x * N_Z + z) * N_C + c + other * (1 - 2 * c)
    at = (lax.axis_index("rep") + away) % N_REP * QUARTER
    lane = lax.broadcasted_iota(jnp.int32, (1, HALF), 1)
    return jnp.concatenate(
        [
            (group * BPG + hot_ref[slot]) * BLK + at + h * HALF + lane
            for h in range(half, half + halves)
            for slot in range(HOT_GRP)
        ],
        axis=1,
    )


PLACES = ((0, 0, 2), (3, 0, 2), (1, 0, 2), (2, 0, 1), (2, 1, 1))


def fold(op, s):
    return functools.reduce(op, [s[:, i : i + 128] for i in range(0, s.shape[1], 128)])


def attend_kernel(q_ref, len_ref, hot_ref, hot_other_ref, *refs):
    n = len(PLACES)
    key_refs, outs = refs[: N_C * n], refs[N_C * n :]
    q = q_ref[...]
    lens = visible_lengths(len_ref, q.shape[0])
    parts = []
    all_scores = []
    for other, hot in enumerate((hot_ref, hot_other_ref)):
        keys = key_refs[other * n : (other + 1) * n]
        scores = []
        for k_ref, place in zip(keys, PLACES):
            numbers = row_numbers(hot, other, *place)
            s = jnp.dot(q, k_ref[...], preferred_element_type=f32)
            scores.append(jnp.where(numbers < lens, s, NEVER))
        all_scores.append(scores)
    for other in range(2):
        keys = key_refs[other * n : (other + 1) * n]
        scores = all_scores[other]
        peak = functools.reduce(jnp.maximum, [fold(jnp.maximum, s) for s in scores])
        peak = peak.max(axis=1, keepdims=True)
        total = 0.0
        numer = None
        for s, k_ref in zip(scores, keys):
            w = jnp.exp2((s - peak) * (SCALE * LOG2_E)).astype(bf16)
            total = total + fold(jnp.add, w.astype(f32))
            v = lax.dot_general(
                w, k_ref[:LAT, :], (((1,), (1,)), ((), ())), preferred_element_type=f32
            )
            numer = v if numer is None else numer + v
        parts.append((peak, total.sum(axis=1, keepdims=True), numer))
    top = jnp.maximum(parts[0][0], parts[1][0])
    numer, total = 0.0, 0.0
    for peak, t, v in parts:
        f = jnp.where(peak > NEVER / 2, jnp.exp((peak - top) * SCALE), 0.0)
        numer = numer + v * f
        total = total + t * f
    o = (numer * (1.0 / jnp.maximum(total, 1.0))).astype(bf16)
    lanes = lax.broadcasted_iota(jnp.int32, (q.shape[0], 128), 1)
    stats = jnp.where(lanes == 0, top * SCALE, total).T[:2, :]
    rows = o.shape[0] // 2
    for flip, o_ref in enumerate(outs):
        o_ref[:rows, :] = o[flip * rows : (flip + 1) * rows]
        mine = stats[:, flip * rows : (flip + 1) * rows]
        terms = three_terms(mine[0:1]) + three_terms(mine[1:2])
        terms = [t.astype(f32) for t in terms] + [jnp.zeros((STAT_ROWS - 6, rows), f32)]
        o_ref[rows:, :rows] = jnp.concatenate(terms, axis=0).astype(bf16)
        o_ref[rows:, rows:] = jnp.zeros((STAT_ROWS, LAT - rows), bf16)


def merge_kernel(*refs):
    n_in = N_X * 2
    parts, sends, (own_ref, stat_ref) = (
        refs[:n_in],
        refs[n_in : n_in + N_FAR - 1],
        refs[n_in + N_FAR - 1 :],
    )
    rows = parts[0].shape[0] - STAT_ROWS
    tops, totals = [], []
    for p in parts:
        s = p[rows:, :rows].astype(f32)
        tops.append(s[0:1] + s[1:2] + s[2:3])
        totals.append(s[3:4] + s[4:5] + s[5:6])
    top = functools.reduce(jnp.maximum, tops)
    weights = [t * jnp.exp(m - top) for m, t in zip(tops, totals)]
    total = sum(weights)
    inv = 1.0 / jnp.maximum(total, 1.0)
    table = [w * inv for w in weights] + [top, total]
    table.append(jnp.zeros((128 - len(table), rows), f32))
    table = jnp.concatenate(table, axis=0).T
    n = rows // N_FAR
    lane = lax.broadcasted_iota(jnp.int32, (n, 128), 1)
    for far in range(N_FAR):
        at = slice(far * n, (far + 1) * n)
        acc = 0.0
        for i, p in enumerate(parts):
            acc = acc + p[at, :].astype(f32) * table[at, i : i + 1]
        if far:
            ref = sends[far - 1]
            ref[:, :LAT] = acc.astype(bf16)
            packed = jnp.zeros((n, 128), f32)
            terms = three_terms(table[at, n_in : n_in + 1])
            terms += three_terms(table[at, n_in + 1 : n_in + 2])
            for i, term in enumerate(terms):
                packed = jnp.where(lane == i, term.astype(f32), packed)
            ref[:, LAT:] = packed.astype(bf16)
        else:
            own_ref[...] = acc
            stat_ref[...] = table[at]


def finish_kernel(own_ref, stat_ref, *refs):
    parts, out_ref = refs[:-1], refs[-1]
    n_in = N_X * 2
    tops, totals, values = [stat_ref[:, n_in : n_in + 1]], [stat_ref[:, n_in + 1 : n_in + 2]], [own_ref[...]]
    for p in parts:
        s = p[:, LAT:].astype(f32)
        tops.append(s[:, 0:1] + s[:, 1:2] + s[:, 2:3])
        totals.append(s[:, 3:4] + s[:, 4:5] + s[:, 5:6])
        values.append(p[:, :LAT].astype(f32))
    top = functools.reduce(jnp.maximum, tops)
    weights = [t * jnp.exp(m - top) for m, t in zip(tops, totals)]
    total = sum(weights)
    o = sum(v * w for v, w in zip(values, weights)) / total
    count = out_ref.shape[0]
    for head in range(o.shape[0] // count):
        out_ref[:, head * LAT : (head + 1) * LAT] = o[head * count : (head + 1) * count].astype(bf16)


def call(kernel, outs, in_specs, args, mib=16, **more):
    return pl.pallas_call(
        kernel,
        out_shape=tuple(jax.ShapeDtypeStruct(*o) for o in outs),
        in_specs=in_specs,
        out_specs=(VMEM,) * len(outs),
        compiler_params=pltpu.CompilerParams(vmem_limit_bytes=mib * MIB),
        **more,
    )(*args)


def on_device(latents, queries, hot_ids, lengths):
    by_column = latents.T
    count = queries.shape[0]
    chunk, pair = ((WIDTH, CHUNK), bf16), ((WIDTH, PAIR), bf16)

    up, down = call(
        first_cut_kernel,
        [pair, pair],
        [SMEM, ANY],
        [hot_ids, by_column],
        mib=50,
        scratch_shapes=[pltpu.SemaphoreType.DMA((4,))],
    )
    up, down = shift_rep(up, 1), shift_rep(down, -1)
    own = queries.reshape(count, -1, WIDTH).transpose(1, 0, 2).reshape(-1, WIDTH)
    near = jnp.concatenate([own, cross_z(own, 4)], axis=0)
    hot_other = swap_core(hot_ids)
    right_a, right_b, left_a, left_b, mine = call(
        own_cut_kernel,
        [pair] * 4 + [chunk],
        [SMEM, ANY],
        [hot_ids, by_column],
        mib=50,
        scratch_shapes=[pltpu.SemaphoreType.DMA((12,))],
    )
    from_left_b, from_right_a = shift_rep(right_b, 1), shift_rep(left_a, -1)
    up, down, near, hot_other = lax.optimization_barrier((up, down, near, hot_other))
    right_a, left_b = call(
        pass_on_kernel,
        [pair] * 2,
        [SMEM] + [VMEM] * 4,
        [hot_ids, up, down, right_a, left_b],
    )
    from_left_a, from_right_b = shift_rep(right_a, 1), shift_rep(left_b, -1)
    for bits in (2, 1):
        near = jnp.concatenate([near, cross_z(near, bits)], axis=0)
    (mine,) = call(
        settle_kernel,
        [chunk],
        [SMEM] + [VMEM] * 5,
        [hot_ids, from_left_a, from_left_b, from_right_a, from_right_b, mine],
    )
    asked = [near] + [cross_x(near, bits) for bits in range(1, N_X)]

    of_left, of_right = shift_rep(mine, 1), shift_rep(mine, -1)
    far_a, far_b = shift_rep(of_left[:, :PAIR], 1), shift_rep(of_right[:, PAIR:], -1)
    far_a, far_b, *asked = lax.optimization_barrier((far_a, far_b, *asked))
    keys = [mine, of_left, of_right, far_a, far_b]
    keys = keys + [swap_core(k) for k in keys]

    rows = near.shape[0] // 2
    part = ((rows + STAT_ROWS, LAT), bf16)
    parts = []
    for i, hop in enumerate((2, 1, 3, 0)):
        if i > 1:
            lengths, *sent = lax.optimization_barrier((lengths, *parts[2 * i - 4 : 2 * i - 2]))
            parts[2 * i - 4 : 2 * i - 2] = sent
        same, flipped = call(
            attend_kernel,
            [part, part],
            [VMEM, SMEM, SMEM, SMEM] + [VMEM] * len(keys),
            [asked[hop], lengths, hot_ids, hot_other, *keys],
        )
        lengths, same, flipped = lax.optimization_barrier((lengths, same, flipped))
        if hop == 0:
            flipped, *sent = lax.optimization_barrier((flipped, *parts[2 * i - 2 :]))
            parts[2 * i - 2 :] = sent
        parts.append(cross_xz(flipped, hop, 1))
        parts.append(cross_xz(same, hop, 0) if hop else same)

    n = own.shape[0]
    message = ((n, LAT + 128), bf16)
    *sends, ours, stat = call(
        merge_kernel,
        [message] * (N_FAR - 1) + [((n, LAT), f32), ((n, 128), f32)],
        [VMEM] * len(parts),
        parts,
    )
    sends = [cross_z(s, bits) for s, bits in zip(sends, Z_ORDER[1:])]
    (out,) = call(
        finish_kernel,
        [((count, n // count * LAT), bf16)],
        [VMEM] * (2 + len(sends)),
        [ours, stat, *sends],
    )
    return out


def solution(mesh):
    assert dict(mesh.shape) == {"ctx": N_X * N_Z * N_C, "rep": N_REP}
    split = Mesh(mesh.devices.reshape(N_X, N_Z, N_C, N_REP), ("x", "z", "c", "rep"))
    ctx = ("x", "z", "c")
    placed = (P((*ctx, "rep"), None), P("rep", ctx), P(ctx), P("rep"))
    return jax.shard_map(
        on_device, mesh=split, in_specs=placed, out_specs=P("rep", ctx), check_vma=False
    )
```

```python
import functools

import jax
import jax.numpy as jnp
from jax import lax
from jax.experimental import pallas as pl
from jax.experimental.pallas import tpu as pltpu
from jax.sharding import Mesh, PartitionSpec as P

H = 128
LAT = 512
ROPE = 64
QK = 192
BLK = 1024
HOT_GRP = 2
BPG = 16
WIDTH = LAT + ROPE
N_X = 4
N_Z = 8
N_C = 2
N_REP = 4
PER_DEV = BPG // N_REP
QUARTER = BLK // N_REP
HALF = QUARTER // 2
PAIR = HOT_GRP * HALF
CHUNK = 2 * PAIR
NEVER = -1e30
STAT_ROWS = 8
Z_ORDER = (0, 4, 2, 6, 1, 5, 3, 7)
SCALE = QK**-0.5
LOG2_E = 1.4426950408889634
N_FAR = N_Z // 2
f32 = jnp.float32
bf16 = jnp.bfloat16

VMEM = pl.BlockSpec(memory_space=pltpu.VMEM)
SMEM = pl.BlockSpec(memory_space=pltpu.SMEM)
ANY = pl.BlockSpec(memory_space=pltpu.HBM)
MIB = 1024 * 1024


def shift_rep(a, by):
    return lax.ppermute(a, "rep", [(i, (i + by) % N_REP) for i in range(N_REP)])


def swap_core(a):
    return lax.ppermute(a, "c", [(0, 1), (1, 0)])


def cross_x(a, bits):
    return lax.ppermute(a, "x", [(i, i ^ bits) for i in range(N_X)])


def cross_z(a, bits):
    return lax.ppermute(a, "z", [(i, i ^ bits) for i in range(N_Z)])


def column(hot_ref, slot, rank, half):
    at = hot_ref[slot] % PER_DEV * BLK + rank * QUARTER + half * HALF
    return pl.ds(pl.multiple_of(at, HALF), HALF)


def run_copies(copies):
    for c in copies:
        c.start()
    for c in copies:
        c.wait()


def first_cut_kernel(hot_ref, lat_ref, up_ref, down_ref, sems):
    far = (lax.axis_index("rep") + 2) % N_REP
    copies = []
    for half, dst in enumerate((up_ref, down_ref)):
        for slot in range(HOT_GRP):
            copies.append(
                pltpu.make_async_copy(
                    lat_ref.at[:, column(hot_ref, slot, far, half)],
                    dst.at[:, pl.ds(slot * HALF, HALF)],
                    sems.at[len(copies)],
                )
            )
    run_copies(copies)


def own_cut_kernel(hot_ref, lat_ref, right_a, right_b, left_a, left_b, mine_ref, sems):
    rank = lax.axis_index("rep")
    copies = []
    for hop, halves in ((1, (right_a, right_b)), (3, (left_a, left_b)), (0, (mine_ref, mine_ref))):
        for half, dst in enumerate(halves):
            for slot in range(HOT_GRP):
                to = slot * HALF + (half * PAIR if hop == 0 else 0)
                copies.append(
                    pltpu.make_async_copy(
                        lat_ref.at[:, column(hot_ref, slot, (rank + hop) % N_REP, half)],
                        dst.at[:, pl.ds(to, HALF)],
                        sems.at[len(copies)],
                    )
                )
    run_copies(copies)


def pass_on_kernel(hot_ref, from_left, from_right, right_in, left_in, right_ref, left_ref):
    rank = lax.axis_index("rep")
    for slot in range(HOT_GRP):
        a = slice(slot * HALF, (slot + 1) * HALF)
        here = hot_ref[slot] // PER_DEV == rank

        @pl.when(here)
        def _():
            right_ref[:, a] = right_in[:, a]
            left_ref[:, a] = left_in[:, a]

        @pl.when(jnp.logical_not(here))
        def _():
            right_ref[:, a] = from_left[:, a]
            left_ref[:, a] = from_right[:, a]


def settle_kernel(hot_ref, left_a, left_b, right_a, right_b, mine_in, mine_ref):
    rank = lax.axis_index("rep")
    for slot in range(HOT_GRP):
        a = slice(slot * HALF, (slot + 1) * HALF)
        b = slice(PAIR + slot * HALF, PAIR + (slot + 1) * HALF)
        away = (hot_ref[slot] // PER_DEV - rank + N_REP) % N_REP

        @pl.when(away == 0)
        def _():
            mine_ref[:, a] = mine_in[:, a]
            mine_ref[:, b] = mine_in[:, b]

        @pl.when(away >= 2)
        def _():
            mine_ref[:, a] = left_a[:, a]

        @pl.when(away == 1)
        def _():
            mine_ref[:, a] = right_a[:, a]

        @pl.when(away == 3)
        def _():
            mine_ref[:, b] = left_b[:, a]

        @pl.when((away == 1) | (away == 2))
        def _():
            mine_ref[:, b] = right_b[:, a]


def three_terms(v):
    hi = v.astype(bf16)
    mid = (v - hi.astype(f32)).astype(bf16)
    low = (v - hi.astype(f32) - mid.astype(f32)).astype(bf16)
    return [hi, mid, low]


def visible_lengths(len_ref, rows):
    count = len_ref.shape[0]
    line = lax.broadcasted_iota(jnp.int32, (count, 1), 0)
    lens = jnp.zeros((count, 1), jnp.int32)
    for i in range(count):
        lens = jnp.where(line == i, len_ref[i], lens)
    return jnp.concatenate([lens] * (rows // count), axis=0)


def row_numbers(hot_ref, other, away, half, halves):
    x, z, c = lax.axis_index("x"), lax.axis_index("z"), lax.axis_index("c")
    group = (x * N_Z + z) * N_C + c + other * (1 - 2 * c)
    at = (lax.axis_index("rep") + away) % N_REP * QUARTER
    lane = lax.broadcasted_iota(jnp.int32, (1, HALF), 1)
    return jnp.concatenate(
        [
            (group * BPG + hot_ref[slot]) * BLK + at + h * HALF + lane
            for h in range(half, half + halves)
            for slot in range(HOT_GRP)
        ],
        axis=1,
    )


PLACES = ((0, 0, 2), (3, 0, 2), (1, 0, 2), (2, 0, 1), (2, 1, 1))


def fold(op, s):
    return functools.reduce(op, [s[:, i : i + 128] for i in range(0, s.shape[1], 128)])


def attend_kernel(q_ref, len_ref, hot_ref, hot_other_ref, *refs):
    n = len(PLACES)
    key_refs, o_ref = refs[:-1], refs[-1]
    q = q_ref[...]
    lens = visible_lengths(len_ref, q.shape[0])
    parts = []
    all_scores = []
    for other, hot in enumerate((hot_ref, hot_other_ref)):
        keys = key_refs[other * n : (other + 1) * n]
        scores = []
        for k_ref, place in zip(keys, PLACES):
            numbers = row_numbers(hot, other, *place)
            s = jnp.dot(q, k_ref[...], preferred_element_type=f32)
            scores.append(jnp.where(numbers < lens, s, NEVER))
        all_scores.append(scores)
    for other in range(2):
        keys = key_refs[other * n : (other + 1) * n]
        scores = all_scores[other]
        peak = functools.reduce(jnp.maximum, [fold(jnp.maximum, s) for s in scores])
        peak = peak.max(axis=1, keepdims=True)
        total = 0.0
        numer = None
        for s, k_ref in zip(scores, keys):
            w = jnp.exp2((s - peak) * (SCALE * LOG2_E)).astype(bf16)
            total = total + fold(jnp.add, w.astype(f32))
            v = lax.dot_general(
                w, k_ref[:LAT, :], (((1,), (1,)), ((), ())), preferred_element_type=f32
            )
            numer = v if numer is None else numer + v
        parts.append((peak, total.sum(axis=1, keepdims=True), numer))
    top = jnp.maximum(parts[0][0], parts[1][0])
    numer, total = 0.0, 0.0
    for peak, t, v in parts:
        f = jnp.where(peak > NEVER / 2, jnp.exp((peak - top) * SCALE), 0.0)
        numer = numer + v * f
        total = total + t * f
    o = (numer * (1.0 / jnp.maximum(total, 1.0))).astype(bf16)
    rows = q.shape[0]
    lanes = lax.broadcasted_iota(jnp.int32, (rows, 128), 1)
    stats = jnp.where(lanes == 0, top * SCALE, total).T[:2, :]
    terms = three_terms(stats[0:1]) + three_terms(stats[1:2])
    terms = [t.astype(f32) for t in terms] + [jnp.zeros((STAT_ROWS - 6, rows), f32)]
    o_ref[:rows, :] = o
    o_ref[rows:, :rows] = jnp.concatenate(terms, axis=0).astype(bf16)
    o_ref[rows:, rows:] = jnp.zeros((STAT_ROWS, LAT - rows), bf16)


def merge_kernel(*refs):
    parts, outs = refs[:N_X], refs[N_X:]
    rows = parts[0].shape[0] - STAT_ROWS
    tops, totals = [], []
    for p in parts:
        s = p[rows:, :rows].astype(f32)
        tops.append(s[0:1] + s[1:2] + s[2:3])
        totals.append(s[3:4] + s[4:5] + s[5:6])
    top = functools.reduce(jnp.maximum, tops)
    weights = [t * jnp.exp(m - top) for m, t in zip(tops, totals)]
    total = sum(weights)
    inv = 1.0 / jnp.maximum(total, 1.0)
    table = [w * inv for w in weights] + [top, total]
    table.append(jnp.zeros((128 - len(table), rows), f32))
    table = jnp.concatenate(table, axis=0).T
    n = rows // N_Z
    lane = lax.broadcasted_iota(jnp.int32, (n, 128), 1)
    for i, ref in enumerate(outs):
        at = slice(i * n, (i + 1) * n)
        acc = 0.0
        for j, p in enumerate(parts):
            acc = acc + p[at, :].astype(f32) * table[at, j : j + 1]
        ref[:, :LAT] = acc.astype(ref.dtype)
        packed = jnp.zeros((n, 128), f32)
        terms = three_terms(table[at, N_X : N_X + 1])
        terms += three_terms(table[at, N_X + 1 : N_X + 2])
        for j, term in enumerate(terms):
            packed = jnp.where(lane == j, term.astype(f32), packed)
        ref[:, LAT:] = packed.astype(ref.dtype)


def finish_kernel(*refs):
    parts, out_ref = [r[...].astype(f32) for r in refs[:-1]], refs[-1]
    tops, totals = [], []
    for p in parts:
        s = p[:, LAT:]
        tops.append(s[:, 0:1] + s[:, 1:2] + s[:, 2:3])
        totals.append(s[:, 3:4] + s[:, 4:5] + s[:, 5:6])
    top = functools.reduce(jnp.maximum, tops)
    weights = [t * jnp.exp(m - top) for m, t in zip(tops, totals)]
    o = sum(p[:, :LAT] * w for p, w in zip(parts, weights)) / sum(weights)
    count = out_ref.shape[0]
    for head in range(o.shape[0] // count):
        out_ref[:, head * LAT : (head + 1) * LAT] = o[head * count : (head + 1) * count].astype(bf16)


def call(kernel, outs, in_specs, args, mib=16, **more):
    return pl.pallas_call(
        kernel,
        out_shape=tuple(jax.ShapeDtypeStruct(*o) for o in outs),
        in_specs=in_specs,
        out_specs=(VMEM,) * len(outs),
        compiler_params=pltpu.CompilerParams(vmem_limit_bytes=mib * MIB),
        **more,
    )(*args)


def on_device(latents, queries, hot_ids, lengths):
    by_column = latents.T
    count = queries.shape[0]
    chunk, pair = ((WIDTH, CHUNK), bf16), ((WIDTH, PAIR), bf16)

    up, down = call(
        first_cut_kernel,
        [pair, pair],
        [SMEM, ANY],
        [hot_ids, by_column],
        mib=50,
        scratch_shapes=[pltpu.SemaphoreType.DMA((4,))],
    )
    up, down = shift_rep(up, 1), shift_rep(down, -1)
    own = queries.reshape(count, -1, WIDTH).transpose(1, 0, 2).reshape(-1, WIDTH)
    near = jnp.concatenate([own, cross_z(own, 4)], axis=0)
    hot_other = swap_core(hot_ids)
    right_a, right_b, left_a, left_b, mine = call(
        own_cut_kernel,
        [pair] * 4 + [chunk],
        [SMEM, ANY],
        [hot_ids, by_column],
        mib=50,
        scratch_shapes=[pltpu.SemaphoreType.DMA((12,))],
    )
    from_left_b, from_right_a = shift_rep(right_b, 1), shift_rep(left_a, -1)
    up, down, near, hot_other = lax.optimization_barrier((up, down, near, hot_other))
    right_a, left_b = call(
        pass_on_kernel,
        [pair] * 2,
        [SMEM] + [VMEM] * 4,
        [hot_ids, up, down, right_a, left_b],
    )
    from_left_a, from_right_b = shift_rep(right_a, 1), shift_rep(left_b, -1)
    for bits in (2, 1):
        near = jnp.concatenate([near, cross_z(near, bits)], axis=0)
    (mine,) = call(
        settle_kernel,
        [chunk],
        [SMEM] + [VMEM] * 5,
        [hot_ids, from_left_a, from_left_b, from_right_a, from_right_b, mine],
    )
    asked = [near] + [cross_x(near, bits) for bits in range(1, N_X)]

    of_left, of_right = shift_rep(mine, 1), shift_rep(mine, -1)
    far_a, far_b = shift_rep(of_left[:, :PAIR], 1), shift_rep(of_right[:, PAIR:], -1)
    far_a, far_b, *asked = lax.optimization_barrier((far_a, far_b, *asked))
    keys = [mine, of_left, of_right, far_a, far_b]
    keys = keys + [swap_core(k) for k in keys]

    rows = near.shape[0]
    parts = []
    for i, hop in enumerate((1, 3, 2, 0)):
        if i > 1:
            lengths, parts[i - 2] = lax.optimization_barrier((lengths, parts[i - 2]))
        (o,) = call(
            attend_kernel,
            [((rows + STAT_ROWS, LAT), bf16)],
            [VMEM, SMEM, SMEM, SMEM] + [VMEM] * len(keys),
            [asked[hop], lengths, hot_ids, hot_other, *keys],
        )
        lengths, o = lax.optimization_barrier((lengths, o))
        parts.append(cross_x(o, hop) if hop else o)

    n = own.shape[0]
    ours, *sends = call(
        merge_kernel,
        [((n, LAT + 128), f32 if i == 0 else bf16) for i in range(N_Z)],
        [VMEM] * N_X,
        parts,
    )
    sends = [cross_z(s, bits) for s, bits in zip(sends, Z_ORDER[1:])]
    (out,) = call(
        finish_kernel,
        [((count, n // count * LAT), bf16)],
        [VMEM] * N_Z,
        [ours, *sends],
    )
    return out


def solution(mesh):
    assert dict(mesh.shape) == {"ctx": N_X * N_Z * N_C, "rep": N_REP}
    split = Mesh(mesh.devices.reshape(N_X, N_Z, N_C, N_REP), ("x", "z", "c", "rep"))
    ctx = ("x", "z", "c")
    placed = (P((*ctx, "rep"), None), P("rep", ctx), P(ctx), P("rep"))
    return jax.shard_map(
        on_device, mesh=split, in_specs=placed, out_specs=P("rep", ctx), check_vma=False
    )
```

```python
import functools

import jax
import jax.numpy as jnp
from jax import lax
from jax.experimental import pallas as pl
from jax.experimental.pallas import tpu as pltpu
from jax.sharding import Mesh, PartitionSpec as P

H = 128
LAT = 512
ROPE = 64
QK = 192
BLK = 1024
HOT_GRP = 2
BPG = 16
WIDTH = LAT + ROPE
N_X = 4
N_Z = 8
N_C = 2
N_REP = 4
PER_DEV = BPG // N_REP
QUARTER = BLK // N_REP
HALF = QUARTER // 2
PAIR = HOT_GRP * HALF
CHUNK = 2 * PAIR
NEVER = -1e30
STAT_ROWS = 8
Z_ORDER = (0, 4, 2, 6, 1, 5, 3, 7)
SCALE = QK**-0.5
LOG2_E = 1.4426950408889634
N_FAR = N_Z // 2
f32 = jnp.float32
bf16 = jnp.bfloat16

VMEM = pl.BlockSpec(memory_space=pltpu.VMEM)
SMEM = pl.BlockSpec(memory_space=pltpu.SMEM)
ANY = pl.BlockSpec(memory_space=pltpu.HBM)
MIB = 1024 * 1024


def shift_rep(a, by):
    return lax.ppermute(a, "rep", [(i, (i + by) % N_REP) for i in range(N_REP)])


def swap_core(a):
    return lax.ppermute(a, "c", [(0, 1), (1, 0)])


def cross_x(a, bits):
    return lax.ppermute(a, "x", [(i, i ^ bits) for i in range(N_X)])


def cross_z(a, bits):
    return lax.ppermute(a, "z", [(i, i ^ bits) for i in range(N_Z)])


def column(hot_ref, slot, rank, half):
    at = hot_ref[slot] % PER_DEV * BLK + rank * QUARTER + half * HALF
    return pl.ds(pl.multiple_of(at, HALF), HALF)


def run_copies(copies):
    for c in copies:
        c.start()
    for c in copies:
        c.wait()


def first_cut_kernel(hot_ref, lat_ref, up_ref, down_ref, sems):
    far = (lax.axis_index("rep") + 2) % N_REP
    copies = []
    for half, dst in enumerate((up_ref, down_ref)):
        for slot in range(HOT_GRP):
            copies.append(
                pltpu.make_async_copy(
                    lat_ref.at[:, column(hot_ref, slot, far, half)],
                    dst.at[:, pl.ds(slot * HALF, HALF)],
                    sems.at[len(copies)],
                )
            )
    run_copies(copies)


def own_cut_kernel(hot_ref, lat_ref, right_a, right_b, left_a, left_b, mine_ref, sems):
    rank = lax.axis_index("rep")
    copies = []
    for hop, halves in ((1, (right_a, right_b)), (3, (left_a, left_b)), (0, (mine_ref, mine_ref))):
        for half, dst in enumerate(halves):
            for slot in range(HOT_GRP):
                to = slot * HALF + (half * PAIR if hop == 0 else 0)
                copies.append(
                    pltpu.make_async_copy(
                        lat_ref.at[:, column(hot_ref, slot, (rank + hop) % N_REP, half)],
                        dst.at[:, pl.ds(to, HALF)],
                        sems.at[len(copies)],
                    )
                )
    run_copies(copies)


def pass_on_kernel(hot_ref, from_left, from_right, right_in, left_in, right_ref, left_ref):
    rank = lax.axis_index("rep")
    for slot in range(HOT_GRP):
        a = slice(slot * HALF, (slot + 1) * HALF)
        here = hot_ref[slot] // PER_DEV == rank

        @pl.when(here)
        def _():
            right_ref[:, a] = right_in[:, a]
            left_ref[:, a] = left_in[:, a]

        @pl.when(jnp.logical_not(here))
        def _():
            right_ref[:, a] = from_left[:, a]
            left_ref[:, a] = from_right[:, a]


def settle_kernel(hot_ref, left_a, left_b, right_a, right_b, mine_in, mine_ref):
    rank = lax.axis_index("rep")
    for slot in range(HOT_GRP):
        a = slice(slot * HALF, (slot + 1) * HALF)
        b = slice(PAIR + slot * HALF, PAIR + (slot + 1) * HALF)
        away = (hot_ref[slot] // PER_DEV - rank + N_REP) % N_REP

        @pl.when(away == 0)
        def _():
            mine_ref[:, a] = mine_in[:, a]
            mine_ref[:, b] = mine_in[:, b]

        @pl.when(away >= 2)
        def _():
            mine_ref[:, a] = left_a[:, a]

        @pl.when(away == 1)
        def _():
            mine_ref[:, a] = right_a[:, a]

        @pl.when(away == 3)
        def _():
            mine_ref[:, b] = left_b[:, a]

        @pl.when((away == 1) | (away == 2))
        def _():
            mine_ref[:, b] = right_b[:, a]


def three_terms(v):
    hi = v.astype(bf16)
    mid = (v - hi.astype(f32)).astype(bf16)
    low = (v - hi.astype(f32) - mid.astype(f32)).astype(bf16)
    return [hi, mid, low]


def visible_lengths(len_ref, rows):
    count = len_ref.shape[0]
    line = lax.broadcasted_iota(jnp.int32, (count, 1), 0)
    lens = jnp.zeros((count, 1), jnp.int32)
    for i in range(count):
        lens = jnp.where(line == i, len_ref[i], lens)
    return jnp.concatenate([lens] * (rows // count), axis=0)


def row_numbers(hot_ref, other, away, half, halves):
    x, z, c = lax.axis_index("x"), lax.axis_index("z"), lax.axis_index("c")
    group = (x * N_Z + z) * N_C + c + other * (1 - 2 * c)
    at = (lax.axis_index("rep") + away) % N_REP * QUARTER
    lane = lax.broadcasted_iota(jnp.int32, (1, HALF), 1)
    return jnp.concatenate(
        [
            (group * BPG + hot_ref[slot]) * BLK + at + h * HALF + lane
            for h in range(half, half + halves)
            for slot in range(HOT_GRP)
        ],
        axis=1,
    )


NEAR = (0, 3, 1)
FAR = 2


def fold(op, s):
    return functools.reduce(op, [s[:, i : i + 128] for i in range(0, s.shape[1], 128)])


def score_kernel(other, len_ref, hot_ref, *refs):
    q_refs, key_refs, outs = refs[:N_X], refs[N_X : N_X + len(NEAR)], refs[N_X + len(NEAR) :]
    lens = visible_lengths(len_ref, q_refs[0].shape[0])
    rows = [row_numbers(hot_ref, other, away, 0, 2) for away in NEAR]
    for i, q_ref in enumerate(q_refs):
        s_ref, peak_ref = outs[2 * i : 2 * i + 2]
        q = q_ref[...]
        peaks = []
        for j, k_ref in enumerate(key_refs):
            s = jnp.dot(q, k_ref[...], preferred_element_type=f32)
            s = jnp.where(rows[j] < lens, s, NEVER)
            s_ref[:, j * CHUNK : (j + 1) * CHUNK] = s
            peaks.append(fold(jnp.maximum, s))
        peak_ref[...] = functools.reduce(jnp.maximum, peaks)


def attend_kernel(q_ref, *refs):
    n = len(NEAR)
    (s_refs, peak_refs), refs = (refs[0:4:2], refs[1:4:2]), refs[4:]
    (len_ref, *hot_refs), refs = refs[:3], refs[3:]
    key_refs, o_ref = refs[:-1], refs[-1]
    q = q_ref[...]
    lens = visible_lengths(len_ref, q.shape[0])
    last = []
    for other in range(N_C):
        for half in range(2):
            k_ref = key_refs[other * (n + 2) + n + half]
            rows = row_numbers(hot_refs[other], other, FAR, half, 1)
            s = jnp.dot(q, k_ref[...], preferred_element_type=f32)
            last.append(jnp.where(rows < lens, s, NEVER))
    parts = []
    for other in range(N_C):
        keys = key_refs[other * (n + 2) : (other + 1) * (n + 2)]
        scores = [s_refs[other][:, i * CHUNK : (i + 1) * CHUNK] for i in range(n)]
        scores += last[other * 2 : other * 2 + 2]
        peak = peak_refs[other][...]
        for s in last[other * 2 : other * 2 + 2]:
            peak = jnp.maximum(peak, fold(jnp.maximum, s))
        peak = peak.max(axis=1, keepdims=True)
        total = 0.0
        numer = None
        for s, k_ref in zip(scores, keys):
            w = jnp.exp2((s - peak) * (SCALE * LOG2_E)).astype(bf16)
            total = total + fold(jnp.add, w.astype(f32))
            v = lax.dot_general(
                w, k_ref[:LAT, :], (((1,), (1,)), ((), ())), preferred_element_type=f32
            )
            numer = v if numer is None else numer + v
        parts.append((peak, total.sum(axis=1, keepdims=True), numer))
    top = jnp.maximum(parts[0][0], parts[1][0])
    numer, total = 0.0, 0.0
    for peak, t, v in parts:
        f = jnp.where(peak > NEVER / 2, jnp.exp((peak - top) * SCALE), 0.0)
        numer = numer + v * f
        total = total + t * f
    o = (numer * (1.0 / jnp.maximum(total, 1.0))).astype(bf16)
    rows = q.shape[0]
    lanes = lax.broadcasted_iota(jnp.int32, (rows, 128), 1)
    stats = jnp.where(lanes == 0, top * SCALE, total).T[:2, :]
    terms = three_terms(stats[0:1]) + three_terms(stats[1:2])
    terms = [t.astype(f32) for t in terms] + [jnp.zeros((STAT_ROWS - 6, rows), f32)]
    o_ref[:rows, :] = o
    o_ref[rows:, :rows] = jnp.concatenate(terms, axis=0).astype(bf16)
    o_ref[rows:, rows:] = jnp.zeros((STAT_ROWS, LAT - rows), bf16)


def merge_kernel(*refs):
    parts, outs = refs[:N_X], refs[N_X:]
    rows = parts[0].shape[0] - STAT_ROWS
    tops, totals = [], []
    for p in parts:
        s = p[rows:, :rows].astype(f32)
        tops.append(s[0:1] + s[1:2] + s[2:3])
        totals.append(s[3:4] + s[4:5] + s[5:6])
    top = functools.reduce(jnp.maximum, tops)
    weights = [t * jnp.exp(m - top) for m, t in zip(tops, totals)]
    total = sum(weights)
    inv = 1.0 / jnp.maximum(total, 1.0)
    table = [w * inv for w in weights] + [top, total]
    table.append(jnp.zeros((128 - len(table), rows), f32))
    table = jnp.concatenate(table, axis=0).T
    n = rows // N_Z
    lane = lax.broadcasted_iota(jnp.int32, (n, 128), 1)
    for i, ref in enumerate(outs):
        at = slice(i * n, (i + 1) * n)
        acc = 0.0
        for j, p in enumerate(parts):
            acc = acc + p[at, :].astype(f32) * table[at, j : j + 1]
        ref[:, :LAT] = acc.astype(ref.dtype)
        packed = jnp.zeros((n, 128), f32)
        terms = three_terms(table[at, N_X : N_X + 1])
        terms += three_terms(table[at, N_X + 1 : N_X + 2])
        for j, term in enumerate(terms):
            packed = jnp.where(lane == j, term.astype(f32), packed)
        ref[:, LAT:] = packed.astype(ref.dtype)


def finish_kernel(*refs):
    parts, out_ref = [r[...].astype(f32) for r in refs[:-1]], refs[-1]
    tops, totals = [], []
    for p in parts:
        s = p[:, LAT:]
        tops.append(s[:, 0:1] + s[:, 1:2] + s[:, 2:3])
        totals.append(s[:, 3:4] + s[:, 4:5] + s[:, 5:6])
    top = functools.reduce(jnp.maximum, tops)
    weights = [t * jnp.exp(m - top) for m, t in zip(tops, totals)]
    o = sum(p[:, :LAT] * w for p, w in zip(parts, weights)) / sum(weights)
    count = out_ref.shape[0]
    for head in range(o.shape[0] // count):
        out_ref[:, head * LAT : (head + 1) * LAT] = o[head * count : (head + 1) * count].astype(bf16)


def call(kernel, outs, in_specs, args, mib=16, **more):
    return pl.pallas_call(
        kernel,
        out_shape=tuple(jax.ShapeDtypeStruct(*o) for o in outs),
        in_specs=in_specs,
        out_specs=(VMEM,) * len(outs),
        compiler_params=pltpu.CompilerParams(vmem_limit_bytes=mib * MIB),
        **more,
    )(*args)


def on_device(latents, queries, hot_ids, lengths):
    by_column = latents.T
    count = queries.shape[0]
    chunk, pair = ((WIDTH, CHUNK), bf16), ((WIDTH, PAIR), bf16)

    up, down = call(
        first_cut_kernel,
        [pair, pair],
        [SMEM, ANY],
        [hot_ids, by_column],
        mib=50,
        scratch_shapes=[pltpu.SemaphoreType.DMA((4,))],
    )
    up, down = shift_rep(up, 1), shift_rep(down, -1)
    own = queries.reshape(count, -1, WIDTH).transpose(1, 0, 2).reshape(-1, WIDTH)
    near = jnp.concatenate([own, cross_z(own, 4)], axis=0)
    hot_other = swap_core(hot_ids)
    right_a, right_b, left_a, left_b, mine = call(
        own_cut_kernel,
        [pair] * 4 + [chunk],
        [SMEM, ANY],
        [hot_ids, by_column],
        mib=50,
        scratch_shapes=[pltpu.SemaphoreType.DMA((12,))],
    )
    from_left_b, from_right_a = shift_rep(right_b, 1), shift_rep(left_a, -1)
    up, down, near, hot_other = lax.optimization_barrier((up, down, near, hot_other))
    right_a, left_b = call(
        pass_on_kernel,
        [pair] * 2,
        [SMEM] + [VMEM] * 4,
        [hot_ids, up, down, right_a, left_b],
    )
    from_left_a, from_right_b = shift_rep(right_a, 1), shift_rep(left_b, -1)
    for bits in (2, 1):
        near = jnp.concatenate([near, cross_z(near, bits)], axis=0)
    (mine,) = call(
        settle_kernel,
        [chunk],
        [SMEM] + [VMEM] * 5,
        [hot_ids, from_left_a, from_left_b, from_right_a, from_right_b, mine],
    )
    asked = [near] + [cross_x(near, bits) for bits in range(1, N_X)]

    of_left, of_right = shift_rep(mine, 1), shift_rep(mine, -1)
    of_left, of_right, *asked = lax.optimization_barrier((of_left, of_right, *asked))
    far_a, far_b = shift_rep(of_left[:, :PAIR], 1), shift_rep(of_right[:, PAIR:], -1)
    keys = [mine, of_left, of_right]
    swapped = [swap_core(k) for k in keys]
    asked, swapped = lax.optimization_barrier((asked, swapped))

    rows = near.shape[0]
    scores = []
    for other, (hot, some) in enumerate(((hot_ids, keys), (hot_other, swapped))):
        found = call(
            functools.partial(score_kernel, other),
            [((rows, len(NEAR) * CHUNK), f32), ((rows, 128), f32)] * N_X,
            [SMEM, SMEM] + [VMEM] * (N_X + len(NEAR)),
            [lengths, hot, *asked, *some],
        )
        scores.append([found[2 * hop : 2 * hop + 2] for hop in range(N_X)])
    scores, far_a, far_b = lax.optimization_barrier((scores, far_a, far_b))
    keys += [far_a, far_b]
    swapped += [swap_core(far_a), swap_core(far_b)]

    parts = []
    for i, hop in enumerate((1, 3, 2, 0)):
        if i > 1:
            lengths, parts[i - 2] = lax.optimization_barrier((lengths, parts[i - 2]))
        (o,) = call(
            attend_kernel,
            [((rows + STAT_ROWS, LAT), bf16)],
            [VMEM] * 5 + [SMEM] * 3 + [VMEM] * (N_C * len(keys)),
            [asked[hop], *scores[0][hop], *scores[1][hop], lengths, hot_ids, hot_other, *keys, *swapped],
        )
        lengths, o = lax.optimization_barrier((lengths, o))
        parts.append(cross_x(o, hop) if hop else o)

    n = own.shape[0]
    ours, *sends = call(
        merge_kernel,
        [((n, LAT + 128), f32 if i == 0 else bf16) for i in range(N_Z)],
        [VMEM] * N_X,
        parts,
    )
    sends = [cross_z(s, bits) for s, bits in zip(sends, Z_ORDER[1:])]
    (out,) = call(
        finish_kernel,
        [((count, n // count * LAT), bf16)],
        [VMEM] * N_Z,
        [ours, *sends],
    )
    return out


def solution(mesh):
    assert dict(mesh.shape) == {"ctx": N_X * N_Z * N_C, "rep": N_REP}
    split = Mesh(mesh.devices.reshape(N_X, N_Z, N_C, N_REP), ("x", "z", "c", "rep"))
    ctx = ("x", "z", "c")
    placed = (P((*ctx, "rep"), None), P("rep", ctx), P(ctx), P("rep"))
    return jax.shard_map(
        on_device, mesh=split, in_specs=placed, out_specs=P("rep", ctx), check_vma=False
    )
```
